128 devices in a mesh: rows: 16 (over x, z), cols: 4 (over y), slab: 2 (over core).
Axes of the slice: x: 4, y: 4, z: 4, core: 2. Of those that a mesh axis runs over, the one named last changes fastest.
Arguments:
- density_blocks: bfloat16 [8192, 4096], P(('rows', 'cols', 'slab')), may hold values from -6 to 6
- block_owner: int32 [8192, 1], P(('rows', 'cols', 'slab')), may hold values from 0 to 127; in each aligned block of 64 rows (0 to 63, 64 to 127, ...) at most 2 rows name the same one
- block_plane: int32 [8192], P(('rows', 'cols', 'slab')), may hold values from 0 to 7
- block_segment: int32 [8192], P(('rows', 'cols', 'slab')), may hold values from 0 to 7
- block_kinds: int32 [8192, 2], P(('rows', 'cols', 'slab')), may hold values from 0 to 3
- basis: bfloat16 [4, 64, 4096], replicated, may hold values from -1.015625 to 1.015625
- ext_potential: float32 [1024, 4096], P(('rows', 'cols', 'slab')), may hold values from -6 to 6
Outputs:
- density: float32 [1024, 4096], P(('rows', 'cols', 'slab'))
- matrix_blocks: bfloat16 [8192, 4096], P(('rows', 'cols', 'slab'))
The draws below stay inside these ranges and needn't reach their ends.
Inputs may be any that keep to these rules, and one draw needn't show every extreme that they name: `block_owner`: among the blocks of one device no owner is named more than 2 times; some owner is named exactly 2 times.
All inputs are finite; a program needn't handle non-finite values.
Results may differ from the reference program's by a relative error of at most 0.0095.
Values may be sent and summed in bfloat16 or wider, within the bound.
No kernel may reach another device: no remote copies, remote signals or barrier semaphores. Data moves between devices by JAX's collectives and lax.ppermute only.
A program may use at most 128 MiB of HBM per device.

```python
import math
import jax
import jax.numpy as jnp
import numpy as np
from jax import lax

BS = 64
KINDS = 4
CZB = 8
SEGW = 512
NB_DEV = 64
ZDEV = 8
PLANE = 4096
CUBE = 4096
SEGS = 8
CAP = 2
NBLOCKS = 8192
NZ = 1024
DEVICES = 128


def plant(array, stream_key, least, high):
    longest = array.shape.index(max(array.shape))
    spots = []
    for shift in (0, 1):
        where = [jax.random.randint(jax.random.fold_in(stream_key, axis), (), 0, length) for axis, length in enumerate(array.shape)]
        where[longest] = (where[longest] + shift) % array.shape[longest]
        spots.append(tuple(where))
    return array.at[spots[0]].set(least).at[spots[1]].set(high)


def steps_of(own_key, shape, shards, smallest, largest):
    def one(axis_at, parts):
        steps = jax.random.uniform(jax.random.fold_in(jax.random.fold_in(own_key, 6), axis_at), (parts,), jnp.float32, smallest / len(shards), largest / len(shards))
        return jnp.repeat(jnp.exp(steps), shape[axis_at] // parts).reshape((-1,) + (1,) * (len(shape) - axis_at - 1))

    gain = one(*shards[0])
    for cut in shards[1:]:
        gain = gain * one(*cut)
    return gain


def routed_block(rng, own, number, rows, amount, top, bound, slope):
    sequence = jax.random.permutation(rng, amount)
    crowded, ordinary = load_shares(amount, rows * top, bound, slope, True), load_shares(amount, rows * top, bound, slope, False)
    places = jnp.arange(amount)

    def named(tallies, turn):
        used = int((tallies > 0).sum())
        fixed = max(1, used // 4)
        moved = fixed + (places - fixed + turn * (used - fixed)) % max(1, amount - fixed)
        return jnp.zeros((amount,), jnp.int32).at[sequence[jnp.where(places < fixed, places, moved)]].set(jnp.asarray(tallies, jnp.int32))

    tallies = jnp.where(number % 4 == 0, named(crowded, number // 4), named(ordinary, number - number // 4 - 1))
    mixed = jax.random.permutation(jax.random.fold_in(own, 3), amount)
    donor, sink = mixed[0:amount // 2 * 2:2], mixed[1:amount // 2 * 2:2]
    margin = jnp.minimum(tallies[donor] - 1, bound - tallies[sink]) // 2
    margin = jnp.where((donor == sequence[0]) | (sink == sequence[0]) | (tallies[sink] == 0), 0, jnp.maximum(margin, 0))
    moved = jax.random.randint(jax.random.fold_in(own, 4), (amount // 2,), 0, 1 << 20) % (margin + 1)
    tallies = tallies.at[donor].add(-moved).at[sink].add(moved)
    members = jnp.searchsorted(jnp.cumsum(tallies), jnp.arange(rows * top), side="right").astype(jnp.int32)
    table = members.reshape(top, rows).T
    table = table[jax.random.permutation(jax.random.fold_in(own, 1), rows)]
    turn = jax.random.randint(jax.random.fold_in(own, 2), (rows, 1), 0, top)
    return jnp.take_along_axis(table, (jnp.arange(top)[None, :] + turn) % top, axis=1)


def load_shares(amount, total, most, slope, full):
    weights = [(1 << 20) // math.isqrt(rank ** slope) + 1 for rank in range(1, amount + 1)]
    largest = most if full else min(most, max(-(-total // amount), total * weights[0] // sum(weights)))
    least = 1 if total - largest >= amount - 1 else 0
    given, surplus = [largest] + [least] * (amount - 1), total - largest - least * (amount - 1)
    while surplus > 0:
        free = [i for i in range(1, amount) if given[i] < largest] or [i for i in range(1, amount) if given[i] < most]
        pool, budget = sum([weights[i] for i in free]), surplus
        for i in free:
            more = min(most - given[i], max(1, budget * weights[i] // pool), surplus)
            given[i] = given[i] + more
            surplus = surplus - more
    return np.array(given)


def gaussian(key, extent, width, reach, pieces=(), kind=jnp.bfloat16):
    entries = jax.random.normal(key, extent, jnp.float32) * width
    if len(pieces) > 0:
        entries = steps_of(key, extent, pieces, -0.22, 0.18) * entries
    return jnp.clip(entries, min=-reach, max=reach).astype(kind)


def setup_inputs(seed: int = 0) -> dict:
    streams_of = jax.random.split(jax.random.key(seed), 8)
    density_blocks = gaussian(streams_of[0], (NBLOCKS, BS * BS), 1.0, 6.0, ((0, 128),))
    block_owner_keys = jax.random.split(jax.random.fold_in(streams_of[1], 1), NBLOCKS // NB_DEV)
    block_owner_turns = jax.random.permutation(jax.random.fold_in(streams_of[1], 3), NBLOCKS // NB_DEV)
    block_owner = jax.vmap(lambda own, number: routed_block(jax.random.fold_in(streams_of[1], 2), own, number, NB_DEV, DEVICES, 1, CAP, 2))(block_owner_keys, block_owner_turns).reshape((NBLOCKS, 1))
    block_plane = plant(jax.random.randint(streams_of[2], (NBLOCKS,), 0, ZDEV), jax.random.fold_in(streams_of[2], 1), 0, ZDEV - 1).astype(jnp.int32)
    block_segment = plant(jax.random.randint(streams_of[3], (NBLOCKS,), 0, SEGS), jax.random.fold_in(streams_of[3], 1), 0, SEGS - 1).astype(jnp.int32)
    block_kinds = plant(jax.random.randint(streams_of[4], (NBLOCKS, 2), 0, KINDS), jax.random.fold_in(streams_of[4], 1), 0, KINDS - 1).astype(jnp.int32)
    basis = gaussian(streams_of[5], (KINDS, BS, CUBE), (1.36 / BS ** 0.5), 1.015625)
    ext_potential = gaussian(streams_of[6], (NZ, PLANE), 1.0, 6.0, ((0, 128),), jnp.float32)
    return dict(density_blocks=density_blocks, block_owner=block_owner, block_plane=block_plane, block_segment=block_segment, block_kinds=block_kinds, basis=basis, ext_potential=ext_potential)


def reference(density_blocks, block_owner, block_plane, block_segment, block_kinds, basis, ext_potential):
    segs = PLANE // SEGW
    rows_total = NZ * segs
    per_batch = 64
    batch_count = density_blocks.shape[0] // per_batch
    start_plane = (block_owner[:, 0] * ZDEV + block_plane).astype(jnp.int32)
    offsets = jnp.arange(CZB, dtype=jnp.int32)
    row_index = (((start_plane[:, None] + offsets[None, :]) % NZ) * segs + block_segment[:, None]).astype(jnp.int32)
    row_batches = row_index.reshape(batch_count, per_batch, CZB)
    kind_batches = block_kinds.reshape(batch_count, per_batch, 2)
    block_batches = density_blocks.reshape(batch_count, per_batch, BS, BS)

    def deposit(grid_rows, batch_item):
        block_batch, index_batch, kind_pair = batch_item
        row_basis = basis[kind_pair[:, 0]].astype(jnp.float32)
        col_basis = basis[kind_pair[:, 1]].astype(jnp.float32)
        half_product = jnp.einsum("bmn,bnc->bmc", block_batch.astype(jnp.float32), col_basis).astype(jnp.bfloat16)
        half_product = lax.optimization_barrier(half_product).astype(jnp.float32)
        product_tile = jnp.sum(row_basis * half_product, axis=1)
        added = jax.ops.segment_sum(product_tile.reshape(-1, SEGW), index_batch.reshape(-1), num_segments=rows_total)
        return grid_rows + added, None

    grid_rows, _ = lax.scan(deposit, jnp.zeros((rows_total, SEGW), jnp.float32), (block_batches, row_batches, kind_batches))
    density = grid_rows.reshape(NZ, PLANE)
    potential = (ext_potential + 0.5 * density).reshape(rows_total, SEGW)

    def integrate(carry, batch_item):
        index_batch, kind_pair = batch_item
        row_basis = basis[kind_pair[:, 0]].astype(jnp.float32)
        col_basis = basis[kind_pair[:, 1]].astype(jnp.float32)
        pot_tile = potential[index_batch.reshape(-1)].reshape(per_batch, CUBE)
        weighted = (row_basis * pot_tile[:, None, :]).astype(jnp.bfloat16)
        weighted = lax.optimization_barrier(weighted).astype(jnp.float32)
        matrix_tile = jnp.einsum("bmc,bnc->bmn", weighted, col_basis).astype(jnp.bfloat16)
        return carry, matrix_tile.reshape(per_batch, BS * BS)

    _, matrix_tiles = lax.scan(integrate, jnp.zeros((), jnp.float32), (row_batches, kind_batches))
    return density, matrix_tiles.reshape(NBLOCKS, BS * BS)
```

```python
import jax
import jax.numpy as jnp
from jax import lax
from jax.experimental import pallas as pl
from jax.experimental.pallas import tpu as pltpu
from jax.sharding import PartitionSpec as P

AXES = ("rows", "cols", "slab")
F32 = jnp.float32
BF16 = jnp.bfloat16
NB = 64
BS = 64
KINDS = 4
CZB = 8
SEGW = 512
SEGS = 8
DEVS = 128
CELLS = CZB * SEGW
PLANE = SEGS * SEGW
LANES = 128
LPS = SEGW // LANES
GROUP = 8
SENDW = 2 * SEGW + LANES

SMEM = pl.BlockSpec(memory_space=pltpu.SMEM)
VMEM = pl.BlockSpec(memory_space=pltpu.VMEM)


def whole(shape):
    return pl.BlockSpec(shape, lambda i: (0,) * len(shape))


def tiles_kernel(
    owner, plane, seg, kinds, dens_ref, basis_ref, out_ref, pn, lhs, a32, tiles, idx
):
    i = pl.program_id(0)

    @pl.when(i == 0)
    def _():
        @pl.loop(0, 2 * DEVS)
        def _(o):
            idx[o] = NB

        @pl.loop(0, NB)
        def _(b):
            o = owner[b, 0]
            first = idx[2 * o]
            second = idx[2 * o + 1]
            free = first == NB
            idx[2 * o] = jnp.where(free, b, first)
            idx[2 * o + 1] = jnp.where(free, second, b)

        for j in range(BS // 2):
            x = dens_ref[:, LANES * j : LANES * (j + 1)].astype(F32)
            pn[pl.ds(2 * j, NB, stride=BS), :] = x
            pn[pl.ds(2 * j + 1, NB, stride=BS), :] = pltpu.roll(x, BS, 1)
        low = lax.broadcasted_iota(jnp.int32, (BS, LANES), 1) < BS

        @pl.loop(0, NB)
        def _(b):
            rows = pl.ds(pl.multiple_of(b * BS, BS), BS)
            kb = kinds[b, 1]
            v = jnp.where(low, pn[rows, :], 0.0)
            v = jnp.where(kb % 2 == 1, pltpu.roll(v, BS, 1), v)
            lhs[rows, 0:LANES] = jnp.where(kb < 2, v, 0.0).astype(BF16)
            lhs[rows, LANES : 2 * LANES] = jnp.where(kb < 2, 0.0, v).astype(BF16)

        tiles[pl.ds(NB * CZB, CZB), :] = jnp.zeros((CZB, SEGW), F32)

    a32[...] = basis_ref[...].reshape(KINDS * BS, SEGW).astype(F32)

    @pl.loop(0, NB // GROUP)
    def _(g):
        rows = pl.ds(pl.multiple_of(g * GROUP * BS, GROUP * BS), GROUP * BS)
        half = jnp.dot(
            lhs[rows, :],
            basis_ref[...].reshape(KINDS * BS, SEGW),
            preferred_element_type=F32,
        )
        for t in range(GROUP):
            b = g * GROUP + t
            a = a32[pl.ds(pl.multiple_of(kinds[b, 0] * BS, BS), BS), :]
            part = jnp.sum(a * half[t * BS : (t + 1) * BS], axis=0, keepdims=True)
            tiles[pl.ds(b * CZB + i, 1), :] = part

    @pl.when(i == CZB - 1)
    def _():
        lane = lax.broadcasted_iota(jnp.int32, (CZB, LANES), 1)

        @pl.loop(0, DEVS // 2)
        def _(q):
            rows = pl.ds(pl.multiple_of(q * 16, 16), 16)
            slots = [idx[4 * q + r] for r in range(4)]
            parts = [tiles[pl.ds(pl.multiple_of(b * CZB, CZB), CZB), :] for b in slots]
            codes = []
            for b in slots:
                held = jnp.minimum(b, NB - 1)
                codes.append((plane[held] * SEGS + seg[held]).astype(F32))
            marks = [
                jnp.where(lane == 0, codes[2 * r], jnp.where(lane == 1, codes[2 * r + 1], 0.0))
                for r in range(2)
            ]
            out_ref[rows, 0:SEGW] = jnp.concatenate([parts[0], parts[2]], axis=0).astype(BF16)
            out_ref[rows, SEGW : 2 * SEGW] = jnp.concatenate(
                [parts[1], parts[3]], axis=0
            ).astype(BF16)
            out_ref[rows, 2 * SEGW :] = jnp.concatenate(marks, axis=0).astype(BF16)


def gather_kernel(got_ref, ext_ref, own_ref, rim_ref, half_ref, code_ref, marks, codes, acc, sem):
    marks[...] = got_ref[:, 2 * SEGW :].astype(F32)
    across = marks[pl.ds(0, DEVS, stride=CZB), :].T
    codes[...] = across[0:8, :].astype(jnp.int32)
    copy = pltpu.make_async_copy(codes, code_ref, sem)
    copy.start()
    acc[...] = jnp.zeros_like(acc)
    copy.wait()

    @pl.loop(0, DEVS // 2)
    def _(q):
        rows = pl.ds(pl.multiple_of(q * 16, 16), 16)
        for r in range(2):
            both = got_ref[rows, r * SEGW : (r + 1) * SEGW].astype(F32)
            for t in range(2):
                code = code_ref[r, 2 * q + t]
                p = code // SEGS
                s = code % SEGS
                for l in range(LPS):
                    at = (s * LPS + l, pl.ds(p, CZB), slice(None))
                    acc[at] = acc[at] + both[t * CZB : (t + 1) * CZB, l * LANES : (l + 1) * LANES]

    for l in range(PLANE // LANES):
        cells = slice(l * LANES, (l + 1) * LANES)
        own = acc[l, 0:CZB, :]
        own_ref[:, cells] = own
        rim_ref[:, cells] = acc[l, CZB : 2 * CZB, :]
        half_ref[:, cells] = ext_ref[:, cells] + 0.5 * own


def cubes_kernel(code_ref, own_ref, rim_ref, ext_ref, below_ref, above_ref, dens_ref, out_ref, pot):
    for l in range(PLANE // LANES):
        cells = slice(l * LANES, (l + 1) * LANES)
        density = own_ref[:, cells] + below_ref[:, cells]
        dens_ref[:, cells] = density
        pot[l, 0:CZB, :] = ext_ref[:, cells] + 0.5 * density
        pot[l, CZB : 2 * CZB, :] = above_ref[:, cells] + 0.5 * rim_ref[:, cells]

    @pl.loop(0, DEVS)
    def _(d):
        rows = pl.ds(pl.multiple_of(d * 16, 16), 16)
        c0 = code_ref[0, d]
        c1 = code_ref[1, d]
        for l in range(LPS):
            first = pot[(c0 % SEGS) * LPS + l, pl.ds(c0 // SEGS, CZB), :]
            second = pot[(c1 % SEGS) * LPS + l, pl.ds(c1 // SEGS, CZB), :]
            out_ref[rows, l * LANES : (l + 1) * LANES] = jnp.concatenate(
                [first, second], axis=0
            ).astype(BF16)


def matrix_kernel(owner, kinds, ret_ref, basis_ref, out_ref, acc, pot, vn, seen, base):
    i = pl.program_id(0)

    @pl.when(i == 0)
    def _():
        @pl.loop(0, DEVS)
        def _(o):
            seen[o] = 0

        @pl.loop(0, NB)
        def _(b):
            o = owner[b, 0]
            rank = seen[o]
            seen[o] = rank + 1
            base[b] = b * 16 + rank * CZB
            pot[pl.ds(pl.multiple_of(b * 16, 16), 16), :] = ret_ref[
                pl.ds(pl.multiple_of(o * 16, 16), 16), :
            ].astype(F32)

        acc[...] = jnp.zeros_like(acc)

    @pl.loop(0, NB // GROUP)
    def _(g):
        rows = pl.ds(pl.multiple_of(g * GROUP * BS, GROUP * BS), GROUP * BS)
        parts = []
        for t in range(GROUP):
            b = g * GROUP + t
            cell = jnp.broadcast_to(pot[pl.ds(base[b] + i, 1), :], (BS, SEGW)).astype(BF16)
            parts.append(basis_ref[kinds[b, 0]] * cell)
        weighted = jnp.concatenate(parts, axis=0)
        acc[rows, :] = acc[rows, :] + lax.dot_general(
            weighted,
            basis_ref[...].reshape(KINDS * BS, SEGW),
            (((1,), (1,)), ((), ())),
            preferred_element_type=F32,
        )

    @pl.when(i == CZB - 1)
    def _():
        @pl.loop(0, NB)
        def _(b):
            rows = pl.ds(pl.multiple_of(b * BS, BS), BS)
            kb = kinds[b, 1]
            v = jnp.where(kb < 2, acc[rows, 0:LANES], acc[rows, LANES : 2 * LANES])
            vn[rows, :] = jnp.where(kb % 2 == 1, pltpu.roll(v, BS, 1), v)

        low = lax.broadcasted_iota(jnp.int32, (NB, LANES), 1) < BS
        for j in range(BS // 2):
            even = vn[pl.ds(2 * j, NB, stride=BS), :]
            odd = pltpu.roll(vn[pl.ds(2 * j + 1, NB, stride=BS), :], BS, 1)
            out_ref[:, LANES * j : LANES * (j + 1)] = jnp.where(low, even, odd).astype(BF16)


def make_tiles(owner, plane, seg, kinds, density_blocks, basis):
    return pl.pallas_call(
        tiles_kernel,
        grid=(CZB,),
        in_specs=[
            SMEM,
            SMEM,
            SMEM,
            SMEM,
            whole((NB, BS * BS)),
            pl.BlockSpec((KINDS, BS, SEGW), lambda i: (0, 0, i)),
        ],
        out_specs=whole((DEVS * CZB, SENDW)),
        out_shape=jax.ShapeDtypeStruct((DEVS * CZB, SENDW), BF16),
        scratch_shapes=[
            pltpu.VMEM((NB * BS, LANES), F32),
            pltpu.VMEM((NB * BS, KINDS * BS), BF16),
            pltpu.VMEM((KINDS * BS, SEGW), F32),
            pltpu.VMEM(((NB + 1) * CZB, SEGW), F32),
            pltpu.SMEM((2 * DEVS,), jnp.int32),
        ],
        name="tiles",
    )(owner, plane, seg, kinds, density_blocks, basis)


def gather_tiles(got, ext_potential):
    slab = jax.ShapeDtypeStruct((CZB, PLANE), F32)
    return pl.pallas_call(
        gather_kernel,
        in_specs=[VMEM, VMEM],
        out_specs=[VMEM, VMEM, VMEM, SMEM],
        out_shape=[slab, slab, slab, jax.ShapeDtypeStruct((8, DEVS), jnp.int32)],
        scratch_shapes=[
            pltpu.VMEM((DEVS * CZB, LANES), F32),
            pltpu.VMEM((8, DEVS), jnp.int32),
            pltpu.VMEM((PLANE // LANES, 2 * CZB, LANES), F32),
            pltpu.SemaphoreType.DMA,
        ],
        name="gather_tiles",
    )(got, ext_potential)


def cut_cubes(codes, own, rim, ext_potential, below, above):
    return pl.pallas_call(
        cubes_kernel,
        in_specs=[SMEM] + [VMEM] * 5,
        out_specs=[VMEM, VMEM],
        out_shape=[
            jax.ShapeDtypeStruct((CZB, PLANE), F32),
            jax.ShapeDtypeStruct((DEVS * 16, SEGW), BF16),
        ],
        scratch_shapes=[pltpu.VMEM((PLANE // LANES, 2 * CZB, LANES), F32)],
        name="cut_cubes",
    )(codes, own, rim, ext_potential, below, above)


def make_matrices(owner, kinds, returned, basis):
    return pl.pallas_call(
        matrix_kernel,
        grid=(CZB,),
        in_specs=[
            SMEM,
            SMEM,
            whole((DEVS * 16, SEGW)),
            pl.BlockSpec((KINDS, BS, SEGW), lambda i: (0, 0, i)),
        ],
        out_specs=whole((NB, BS * BS)),
        out_shape=jax.ShapeDtypeStruct((NB, BS * BS), BF16),
        scratch_shapes=[
            pltpu.VMEM((NB * BS, KINDS * BS), F32),
            pltpu.VMEM((NB * 16, SEGW), F32),
            pltpu.VMEM((NB * BS, LANES), F32),
            pltpu.SMEM((DEVS,), jnp.int32),
            pltpu.SMEM((NB,), jnp.int32),
        ],
        name="matrices",
    )(owner, kinds, returned, basis)


def shifted(x, by):
    size = lax.axis_size(AXES)
    return lax.ppermute(x, AXES, [(i, (i + by) % size) for i in range(size)])


def exchanged(x):
    return lax.all_to_all(x, AXES, split_axis=0, concat_axis=0, tiled=True)


def local(
    density_blocks, block_owner, block_plane, block_segment, block_kinds, basis, ext_potential
):
    sent = make_tiles(
        block_owner, block_plane, block_segment, block_kinds, density_blocks, basis
    )
    own, rim, half, codes = gather_tiles(exchanged(sent), ext_potential)
    below = shifted(rim, 1)
    above = shifted(half, -1)
    density, cubes = cut_cubes(codes, own, rim, ext_potential, below, above)
    matrices = make_matrices(block_owner, block_kinds, exchanged(cubes), basis)
    return density, matrices


def solution(mesh):
    rows = P(AXES, None)
    flat = P(AXES)
    return jax.shard_map(
        local,
        mesh=mesh,
        in_specs=(rows, rows, flat, flat, rows, P(), rows),
        out_specs=(rows, rows),
        check_vma=False,
    )
```

```python
import jax
import jax.numpy as jnp
from jax import lax
from jax.experimental import pallas as pl
from jax.experimental.pallas import tpu as pltpu
from jax.sharding import PartitionSpec as P

AXES = ("rows", "cols", "slab")
F32 = jnp.float32
BF16 = jnp.bfloat16
NB = 64
BS = 64
KINDS = 4
CZB = 8
SEGW = 512
SEGS = 8
DEVS = 128
PLANE = SEGS * SEGW
LANES = 128
HALVES = 2
HALF = SEGW // HALVES
LPS = HALF // LANES
STEPS = CZB // 2
GROUP = 32

SMEM = pl.BlockSpec(memory_space=pltpu.SMEM)
VMEM = pl.BlockSpec(memory_space=pltpu.VMEM)


def whole(shape):
    return pl.BlockSpec(shape, lambda i: (0,) * len(shape))


def basis_specs(h):
    def spec(t):
        return pl.BlockSpec((KINDS, BS, HALF), lambda i: (0, 0, (2 * i + t) * HALVES + h))

    return [spec(0), spec(1)]


def cost(flops, moved):
    return pl.CostEstimate(flops=flops, bytes_accessed=moved, transcendentals=0)


def joined(first, second):
    parts = [ref[...].reshape(KINDS * BS, HALF) for ref in (first, second)]
    return jnp.concatenate(parts, axis=1)


def even_rows_first():
    shape = (KINDS * BS, KINDS * BS)
    to = lax.broadcasted_iota(jnp.int32, shape, 0)
    source = lax.broadcasted_iota(jnp.int32, shape, 1)
    row = to & (BS - 1)
    half = BS // 2
    wanted = (to - row) + jnp.where(row < half, 2 * row, 2 * (row - half) + 1)
    return jnp.where(source == wanted, 1.0, 0.0).astype(BF16)


def tiles_kernel(
    h, owner, plane, seg, kinds, dens_ref, first, second, out_ref, pn, lhs, a32, perm, tiles, idx
):
    i = pl.program_id(0)
    pairs = BS // 2

    @pl.when(i == 0)
    def _():
        @pl.loop(0, 2 * DEVS, unroll=16)
        def _(o):
            idx[o] = NB

        @pl.loop(0, NB, unroll=4)
        def _(b):
            o = owner[b, 0]
            was = idx[2 * o]
            after = idx[2 * o + 1]
            free = was == NB
            idx[2 * o] = jnp.where(free, b, was)
            idx[2 * o + 1] = jnp.where(free, after, b)

        perm[...] = even_rows_first()
        pn[...] = dens_ref[...].astype(F32).reshape(NB, pairs, LANES)
        low = lax.broadcasted_iota(jnp.int32, (pairs, LANES), 1) < BS

        @pl.loop(0, NB, unroll=4)
        def _(b):
            rows = pl.ds(pl.multiple_of(b * BS, BS), BS)
            kb = kinds[b, 1]
            odd = (kb & 1) == 1
            v = pn[b]
            r = pltpu.roll(v, BS, 1)
            keep = low != odd
            evens = jnp.where(keep, jnp.where(odd, r, v), 0.0)
            odds = jnp.where(keep, jnp.where(odd, v, r), 0.0)
            v = jnp.concatenate([evens, odds], axis=0)
            lhs[rows, 0:LANES] = jnp.where(kb < 2, v, 0.0).astype(BF16)
            lhs[rows, LANES : 2 * LANES] = jnp.where(kb < 2, 0.0, v).astype(BF16)

        tiles[pl.ds(NB * CZB, CZB), :] = jnp.zeros((CZB, HALF), F32)

    a32[...] = jnp.dot(perm[...], joined(first, second), preferred_element_type=F32)

    @pl.loop(0, NB // GROUP)
    def _(g):
        rows = pl.ds(pl.multiple_of(g * GROUP * BS, GROUP * BS), GROUP * BS)
        half = jnp.dot(lhs[rows, :], joined(first, second), preferred_element_type=F32)
        for t in range(GROUP):
            b = g * GROUP + t
            a = a32[pl.ds(pl.multiple_of(kinds[b, 0] * BS, BS), BS), :]
            part = jnp.sum(a * half[t * BS : (t + 1) * BS], axis=0, keepdims=True)
            tiles[pl.ds(b * CZB + 2 * i, 1), :] = part[:, :HALF]
            tiles[pl.ds(b * CZB + 2 * i + 1, 1), :] = part[:, HALF:]

    @pl.when(i == STEPS - 1)
    def _():
        lane = lax.broadcasted_iota(jnp.int32, (CZB, LANES), 1)

        @pl.loop(0, DEVS // 2, unroll=4)
        def _(q):
            rows = pl.ds(pl.multiple_of(q * 16, 16), 16)
            slots = [idx[4 * q + r] for r in range(4)]
            parts = [tiles[pl.ds(pl.multiple_of(b * CZB, CZB), CZB), :] for b in slots]
            out_ref[rows, 0:HALF] = jnp.concatenate([parts[0], parts[2]], axis=0).astype(BF16)
            out_ref[rows, HALF : 2 * HALF] = jnp.concatenate(
                [parts[1], parts[3]], axis=0
            ).astype(BF16)
            if h == 0:
                codes = []
                for b in slots:
                    held = jnp.minimum(b, NB - 1)
                    codes.append((plane[held] * SEGS + seg[held]).astype(F32))
                marks = [
                    jnp.where(lane == 0, codes[2 * r], jnp.where(lane == 1, codes[2 * r + 1], 0.0))
                    for r in range(2)
                ]
                out_ref[rows, 2 * HALF :] = jnp.concatenate(marks, axis=0).astype(BF16)


def spread(at_ref, got_ref, ext_ref, own_ref, rim_ref, half_ref, acc, h):
    acc[...] = jnp.zeros_like(acc)

    @pl.loop(0, DEVS // 2, unroll=2)
    def _(q):
        rows = pl.ds(pl.multiple_of(q * 16, 16), 16)
        for r in range(2):
            both = got_ref[rows, r * HALF : (r + 1) * HALF].astype(F32)
            for t in range(2):
                p = at_ref[r, 2 * q + t]
                s = at_ref[2 + r, 2 * q + t]
                for l in range(LPS):
                    at = (s + l, pl.ds(p, CZB), slice(None))
                    acc[at] = acc[at] + both[t * CZB : (t + 1) * CZB, l * LANES : (l + 1) * LANES]

    for s in range(SEGS):
        for l in range(LPS):
            n = s * LPS + l
            cells = slice(n * LANES, (n + 1) * LANES)
            grid = slice(s * SEGW + h * HALF + l * LANES, s * SEGW + h * HALF + (l + 1) * LANES)
            own = acc[n, 0:CZB, :]
            own_ref[:, cells] = own
            rim_ref[:, cells] = acc[n, CZB : 2 * CZB, :]
            half_ref[:, cells] = ext_ref[:, grid] + 0.5 * own


def gather_first(got_ref, ext_ref, own_ref, rim_ref, half_ref, at_ref, marks, places, acc, sem):
    marks[...] = got_ref[:, 2 * HALF :].astype(F32)
    across = marks[pl.ds(0, DEVS, stride=CZB), :].T
    codes = across[0:2, :].astype(jnp.int32)
    places[0:2, :] = codes >> 3
    places[2:4, :] = (codes & 7) * LPS
    copy = pltpu.make_async_copy(places, at_ref, sem)
    copy.start()
    copy.wait()
    spread(at_ref, got_ref, ext_ref, own_ref, rim_ref, half_ref, acc, 0)


def gather_second(at_ref, got_ref, ext_ref, own_ref, rim_ref, half_ref, acc):
    spread(at_ref, got_ref, ext_ref, own_ref, rim_ref, half_ref, acc, 1)


def cubes_kernel(h, at_ref, own_ref, rim_ref, ext_ref, below_ref, above_ref, *rest):
    if h == 0:
        dens_ref, out_ref, pot = rest
    else:
        other_ref, dens_ref, out_ref, pot = rest
    for s in range(SEGS):
        for l in range(LPS):
            n = s * LPS + l
            cells = slice(n * LANES, (n + 1) * LANES)
            grid = slice(s * SEGW + h * HALF + l * LANES, s * SEGW + h * HALF + (l + 1) * LANES)
            density = own_ref[:, cells] + below_ref[:, cells]
            if h == 0:
                dens_ref[:, cells] = density
            else:
                dens_ref[:, grid] = density
                dens_ref[:, s * SEGW + l * LANES : s * SEGW + (l + 1) * LANES] = other_ref[:, cells]
            pot[n, 0:CZB, :] = ext_ref[:, grid] + 0.5 * density
            pot[n, CZB : 2 * CZB, :] = above_ref[:, cells] + 0.5 * rim_ref[:, cells]

    @pl.loop(0, DEVS, unroll=4)
    def _(d):
        rows = pl.ds(pl.multiple_of(d * 16, 16), 16)
        for l in range(LPS):
            cubes = [pot[at_ref[2 + r, d] + l, pl.ds(at_ref[r, d], CZB), :] for r in range(2)]
            out_ref[rows, l * LANES : (l + 1) * LANES] = jnp.concatenate(cubes, axis=0).astype(BF16)


def matrix_kernel(h, owner, kinds, ret_ref, first, second, *rest):
    if h == 0:
        out_ref, acc, pot, perm, shuffled, seen, base = rest
    else:
        other_ref, out_ref, acc, pot, perm, shuffled, seen, base, vn = rest
    i = pl.program_id(0)
    pairs = BS // 2

    @pl.when(i == 0)
    def _():
        @pl.loop(0, DEVS, unroll=16)
        def _(o):
            seen[o] = 0

        @pl.loop(0, NB, unroll=4)
        def _(b):
            o = owner[b, 0]
            rank = seen[o]
            seen[o] = rank + 1
            base[b] = b * 16 + rank * CZB
            pot[pl.ds(pl.multiple_of(b * 16, 16), 16), :] = ret_ref[
                pl.ds(pl.multiple_of(o * 16, 16), 16), :
            ].astype(F32)

        perm[...] = even_rows_first()
        acc[...] = jnp.zeros_like(acc)

    shuffled[...] = jnp.dot(
        perm[...], joined(first, second), preferred_element_type=F32
    ).astype(BF16)

    @pl.loop(0, NB // GROUP)
    def _(g):
        rows = pl.ds(pl.multiple_of(g * GROUP * BS, GROUP * BS), GROUP * BS)
        parts = []
        for t in range(GROUP):
            b = g * GROUP + t
            cells = [pot[pl.ds(base[b] + 2 * i + k, 1), :] for k in range(2)]
            cell = jnp.broadcast_to(jnp.concatenate(cells, axis=1), (BS, SEGW)).astype(BF16)
            parts.append(shuffled[pl.ds(pl.multiple_of(kinds[b, 0] * BS, BS), BS), :] * cell)
        weighted = jnp.concatenate(parts, axis=0)
        acc[rows, :] = acc[rows, :] + lax.dot_general(
            weighted,
            joined(first, second),
            (((1,), (1,)), ((), ())),
            preferred_element_type=F32,
        )

    @pl.when(i == STEPS - 1)
    def _():
        low = lax.broadcasted_iota(jnp.int32, (pairs, LANES), 1) < BS

        @pl.loop(0, NB, unroll=4)
        def _(b):
            rows = pl.ds(pl.multiple_of(b * BS, BS), BS)
            kb = kinds[b, 1]
            odd = (kb & 1) == 1
            v = jnp.where(kb < 2, acc[rows, 0:LANES], acc[rows, LANES : 2 * LANES])
            r = pltpu.roll(v, BS, 1)
            evens = jnp.where(odd, r[:pairs], v[:pairs])
            odds = jnp.where(odd, v[pairs:], r[pairs:])
            block = jnp.where(low, evens, odds)
            if h == 0:
                out_ref[b] = block
            else:
                vn[b] = block + other_ref[b]

        if h == 1:
            out_ref[...] = vn[...].reshape(NB, BS * BS).astype(BF16)


def make_tiles(h, owner, plane, seg, kinds, density_blocks, basis):
    width = 2 * HALF + (LANES if h == 0 else 0)
    return pl.pallas_call(
        lambda *refs: tiles_kernel(h, *refs),
        grid=(STEPS,),
        in_specs=[SMEM, SMEM, SMEM, SMEM, whole((NB, BS * BS))] + basis_specs(h),
        out_specs=whole((DEVS * CZB, width)),
        out_shape=jax.ShapeDtypeStruct((DEVS * CZB, width), BF16),
        scratch_shapes=[
            pltpu.VMEM((NB, BS // 2, LANES), F32),
            pltpu.VMEM((NB * BS, KINDS * BS), BF16),
            pltpu.VMEM((KINDS * BS, SEGW), F32),
            pltpu.VMEM((KINDS * BS, KINDS * BS), BF16),
            pltpu.VMEM(((NB + 1) * CZB, HALF), F32),
            pltpu.SMEM((2 * DEVS,), jnp.int32),
        ],
        cost_estimate=cost(2 * NB * BS * KINDS * BS * CZB * HALF, 4 << 20),
        name=f"tiles{h}",
    )(owner, plane, seg, kinds, density_blocks, basis, basis)


def gather_tiles(h, got, ext_potential, places=None):
    part = jax.ShapeDtypeStruct((CZB, PLANE // HALVES), F32)
    acc = pltpu.VMEM((SEGS * LPS, 2 * CZB, LANES), F32)
    if h == 0:
        return pl.pallas_call(
            gather_first,
            in_specs=[VMEM, VMEM],
            out_specs=[VMEM, VMEM, VMEM, SMEM],
            out_shape=[part, part, part, jax.ShapeDtypeStruct((8, DEVS), jnp.int32)],
            scratch_shapes=[
                pltpu.VMEM((DEVS * CZB, LANES), F32),
                pltpu.VMEM((8, DEVS), jnp.int32),
                acc,
                pltpu.SemaphoreType.DMA,
            ],
            cost_estimate=cost(1 << 20, 3 << 20),
            name="gather_tiles0",
        )(got, ext_potential)
    return pl.pallas_call(
        gather_second,
        in_specs=[SMEM, VMEM, VMEM],
        out_specs=[VMEM, VMEM, VMEM],
        out_shape=[part, part, part],
        scratch_shapes=[acc],
        cost_estimate=cost(1 << 20, 3 << 20),
        name="gather_tiles1",
    )(places, got, ext_potential)


def cut_cubes(h, places, own, rim, ext_potential, below, above, *other):
    width = PLANE // HALVES if h == 0 else PLANE
    return pl.pallas_call(
        lambda *refs: cubes_kernel(h, *refs),
        in_specs=[SMEM] + [VMEM] * (5 + len(other)),
        out_specs=[VMEM, VMEM],
        out_shape=[
            jax.ShapeDtypeStruct((CZB, width), F32),
            jax.ShapeDtypeStruct((DEVS * 16, HALF), BF16),
        ],
        scratch_shapes=[pltpu.VMEM((SEGS * LPS, 2 * CZB, LANES), F32)],
        cost_estimate=cost(1 << 20, 3 << 20),
        name=f"cut_cubes{h}",
    )(places, own, rim, ext_potential, below, above, *other)


def make_matrices(h, owner, kinds, returned, basis, *other):
    blocks = (NB, BS // 2, LANES)
    out = (blocks, F32) if h == 0 else ((NB, BS * BS), BF16)
    return pl.pallas_call(
        lambda *refs: matrix_kernel(h, *refs),
        grid=(STEPS,),
        in_specs=[SMEM, SMEM, whole((DEVS * 16, HALF))]
        + basis_specs(h)
        + [whole(blocks)] * len(other),
        out_specs=whole(out[0]),
        out_shape=jax.ShapeDtypeStruct(*out),
        scratch_shapes=[
            pltpu.VMEM((NB * BS, KINDS * BS), F32),
            pltpu.VMEM((NB * 16, HALF), F32),
            pltpu.VMEM((KINDS * BS, KINDS * BS), BF16),
            pltpu.VMEM((KINDS * BS, SEGW), BF16),
            pltpu.SMEM((DEVS,), jnp.int32),
            pltpu.SMEM((NB,), jnp.int32),
        ]
        + [pltpu.VMEM(blocks, F32)] * h,
        cost_estimate=cost(2 * NB * BS * KINDS * BS * CZB * HALF, 4 << 20),
        name=f"matrices{h}",
    )(owner, kinds, returned, basis, basis, *other)


def shifted(x, by):
    size = lax.axis_size(AXES)
    return lax.ppermute(x, AXES, [(i, (i + by) % size) for i in range(size)])


def exchanged(x):
    return lax.all_to_all(x, AXES, split_axis=0, concat_axis=0, tiled=True)


def local(
    density_blocks, block_owner, block_plane, block_segment, block_kinds, basis, ext_potential
):
    sent = [
        make_tiles(h, block_owner, block_plane, block_segment, block_kinds, density_blocks, basis)
        for h in range(HALVES)
    ]
    got = [exchanged(x) for x in sent]

    own0, rim0, half0, places = gather_tiles(0, got[0], ext_potential)
    below0, above0 = shifted(rim0, 1), shifted(half0, -1)
    density0, cubes0 = cut_cubes(0, places, own0, rim0, ext_potential, below0, above0)
    returned0 = exchanged(cubes0)

    own1, rim1, half1 = gather_tiles(1, got[1], ext_potential, places)
    below1, above1 = shifted(rim1, 1), shifted(half1, -1)
    density, cubes1 = cut_cubes(
        1, places, own1, rim1, ext_potential, below1, above1, density0
    )
    returned1 = exchanged(cubes1)

    matrices0 = make_matrices(0, block_owner, block_kinds, returned0, basis)
    matrices = make_matrices(1, block_owner, block_kinds, returned1, basis, matrices0)
    return density, matrices


def solution(mesh):
    rows = P(AXES, None)
    flat = P(AXES)
    return jax.shard_map(
        local,
        mesh=mesh,
        in_specs=(rows, rows, flat, flat, rows, P(), rows),
        out_specs=(rows, rows),
        check_vma=False,
    )
```

```python
import jax
import jax.numpy as jnp
from jax import lax
from jax.experimental import pallas as pl
from jax.experimental.pallas import tpu as pltpu
from jax.sharding import PartitionSpec as P


AXES = ("rows", "cols", "slab")
F32 = jnp.float32
BF16 = jnp.bfloat16
NB = 64
BS = 64
KINDS = 4
CZB = 8
SEGW = 512
SEGS = 8
DEVS = 128
PLANE = SEGS * SEGW
LANES = 128
HALVES = 2
HALF = SEGW // HALVES
LPS = HALF // LANES
STEPS = CZB // 2
GROUP = 64

SMEM = pl.BlockSpec(memory_space=pltpu.SMEM)
VMEM = pl.BlockSpec(memory_space=pltpu.VMEM)


def whole(shape):
    return pl.BlockSpec(shape, lambda i: (0,) * len(shape))


def basis_specs(h):
    def spec(t):
        return pl.BlockSpec((KINDS, BS, HALF), lambda i: (0, 0, (2 * i + t) * HALVES + h))

    return [spec(0), spec(1)]


def cost(flops, moved):
    return pl.CostEstimate(flops=flops, bytes_accessed=moved, transcendentals=0)


def joined(first, second):
    parts = [ref[...].reshape(KINDS * BS, HALF) for ref in (first, second)]
    return jnp.concatenate(parts, axis=1)


def home(slab):
    chip = slab >> 1
    x, zi, yi = chip >> 4, (chip >> 2) & 3, chip & 3
    z = zi + (x & 1) * (3 - 2 * zi)
    y = yi + (zi & 1) * (3 - 2 * yi)
    return (x * 4 + z) * 8 + y * 2 + (slab & 1)


def even_rows_first():
    shape = (KINDS * BS, KINDS * BS)
    to = lax.broadcasted_iota(jnp.int32, shape, 0)
    source = lax.broadcasted_iota(jnp.int32, shape, 1)
    row = to & (BS - 1)
    half = BS // 2
    wanted = (to - row) + jnp.where(row < half, 2 * row, 2 * (row - half) + 1)
    return jnp.where(source == wanted, 1.0, 0.0).astype(BF16)


def tiles_kernel(h, *refs):
    owner, kinds, plane, seg, dens_ref, first, second, out_ref, base = refs[:9]
    pn, lhs, a32, perm, tiles, idx = refs[9:]
    i = pl.program_id(0)
    pairs = BS // 2

    @pl.when(i == 0)
    def _():
        @pl.loop(0, 2 * DEVS, unroll=16)
        def _(o):
            idx[o] = NB

        @pl.loop(0, NB, unroll=4)
        def _(b):
            o = home(owner[0, b])
            was = idx[2 * o]
            after = idx[2 * o + 1]
            free = was == NB
            idx[2 * o] = jnp.where(free, b, was)
            idx[2 * o + 1] = jnp.where(free, after, b)
            base[b] = o * 16 + jnp.where(free, 0, CZB)

        perm[...] = even_rows_first()
        pn[...] = dens_ref[...].astype(F32).reshape(NB, pairs, LANES)
        low = lax.broadcasted_iota(jnp.int32, (pairs, LANES), 1) < BS

        @pl.loop(0, NB, unroll=4)
        def _(b):
            rows = pl.ds(pl.multiple_of(b * BS, BS), BS)
            kb = kinds[1, b]
            odd = (kb & 1) == 1
            v = pn[b]
            r = pltpu.roll(v, BS, 1)
            keep = low != odd
            evens = jnp.where(keep, jnp.where(odd, r, v), 0.0)
            odds = jnp.where(keep, jnp.where(odd, v, r), 0.0)
            v = jnp.concatenate([evens, odds], axis=0)
            lhs[rows, 0:LANES] = jnp.where(kb < 2, v, 0.0).astype(BF16)
            lhs[rows, LANES : 2 * LANES] = jnp.where(kb < 2, 0.0, v).astype(BF16)

        tiles[pl.ds(NB * CZB, CZB), :] = jnp.zeros((CZB, HALF), F32)

    a32[...] = jnp.dot(perm[...], joined(first, second), preferred_element_type=F32)

    @pl.loop(0, NB // GROUP)
    def _(g):
        rows = pl.ds(pl.multiple_of(g * GROUP * BS, GROUP * BS), GROUP * BS)
        half = jnp.dot(lhs[rows, :], joined(first, second), preferred_element_type=F32)
        for t in range(GROUP):
            b = g * GROUP + t
            a = a32[pl.ds(pl.multiple_of(kinds[0, b] * BS, BS), BS), :]
            part = jnp.sum(a * half[t * BS : (t + 1) * BS], axis=0, keepdims=True)
            tiles[pl.ds(b * CZB + 2 * i, 1), :] = part[:, :HALF]
            tiles[pl.ds(b * CZB + 2 * i + 1, 1), :] = part[:, HALF:]

    @pl.when(i == STEPS - 1)
    def _():
        lane = lax.broadcasted_iota(jnp.int32, (CZB, LANES), 1)

        @pl.loop(0, DEVS // 2, unroll=4)
        def _(q):
            rows = pl.ds(pl.multiple_of(q * 16, 16), 16)
            slots = [idx[4 * q + r] for r in range(4)]
            parts = [tiles[pl.ds(pl.multiple_of(b * CZB, CZB), CZB), :] for b in slots]
            out_ref[rows, 0:HALF] = jnp.concatenate([parts[0], parts[2]], axis=0).astype(BF16)
            out_ref[rows, HALF : 2 * HALF] = jnp.concatenate(
                [parts[1], parts[3]], axis=0
            ).astype(BF16)
            if h == 0:
                codes = []
                for b in slots:
                    held = jnp.minimum(b, NB - 1)
                    codes.append((plane[held] * SEGS + seg[held]).astype(F32))
                marks = [
                    jnp.where(lane == 0, codes[2 * r], jnp.where(lane == 1, codes[2 * r + 1], 0.0))
                    for r in range(2)
                ]
                out_ref[rows, 2 * HALF :] = jnp.concatenate(marks, axis=0).astype(BF16)


def spread(at_ref, got_ref, ext_ref, own_ref, rim_ref, half_ref, acc, h):
    acc[...] = jnp.zeros_like(acc)

    @pl.loop(0, DEVS // 2, unroll=2)
    def _(q):
        rows = pl.ds(pl.multiple_of(q * 16, 16), 16)
        for r in range(2):
            both = got_ref[rows, r * HALF : (r + 1) * HALF].astype(F32)
            for t in range(2):
                row = at_ref[r, 2 * q + t]
                for l in range(LPS):
                    at = (pl.ds(row + 2 * CZB * l, CZB), slice(None))
                    acc[at] = acc[at] + both[t * CZB : (t + 1) * CZB, l * LANES : (l + 1) * LANES]

    for s in range(SEGS):
        for l in range(LPS):
            n = s * LPS + l
            cells = slice(n * LANES, (n + 1) * LANES)
            grid = slice(s * SEGW + h * HALF + l * LANES, s * SEGW + h * HALF + (l + 1) * LANES)
            row = 2 * CZB * n
            own = acc[row : row + CZB, :]
            own_ref[:, cells] = own
            rim_ref[:, cells] = acc[row + CZB : row + 2 * CZB, :]
            half_ref[:, cells] = ext_ref[:, grid] + 0.5 * own


def gather_first(got_ref, ext_ref, own_ref, rim_ref, half_ref, at_ref, marks, places, acc, sem):
    marks[...] = got_ref[:, 2 * HALF :].astype(F32)
    across = marks[pl.ds(0, DEVS, stride=CZB), :].T
    codes = across[0:2, :].astype(jnp.int32)
    places[0:2, :] = (codes >> 3) + (codes & 7) * (2 * CZB * LPS)
    copy = pltpu.make_async_copy(places, at_ref, sem)
    copy.start()
    copy.wait()
    spread(at_ref, got_ref, ext_ref, own_ref, rim_ref, half_ref, acc, 0)


def gather_second(at_ref, got_ref, ext_ref, own_ref, rim_ref, half_ref, acc):
    spread(at_ref, got_ref, ext_ref, own_ref, rim_ref, half_ref, acc, 1)


def cubes_kernel(h, at_ref, own_ref, rim_ref, ext_ref, below_ref, above_ref, *rest):
    if h == 0:
        dens_ref, out_ref, pot = rest
    else:
        other_ref, dens_ref, out_ref, pot = rest
    for s in range(SEGS):
        for l in range(LPS):
            n = s * LPS + l
            cells = slice(n * LANES, (n + 1) * LANES)
            grid = slice(s * SEGW + h * HALF + l * LANES, s * SEGW + h * HALF + (l + 1) * LANES)
            density = own_ref[:, cells] + below_ref[:, cells]
            if h == 0:
                dens_ref[:, cells] = density
            else:
                dens_ref[:, grid] = density
                dens_ref[:, s * SEGW + l * LANES : s * SEGW + (l + 1) * LANES] = other_ref[:, cells]
            row = 2 * CZB * n
            pot[row : row + CZB, :] = ext_ref[:, grid] + 0.5 * density
            pot[row + CZB : row + 2 * CZB, :] = above_ref[:, cells] + 0.5 * rim_ref[:, cells]

    @pl.loop(0, DEVS, unroll=4)
    def _(d):
        rows = pl.ds(pl.multiple_of(d * 16, 16), 16)
        for l in range(LPS):
            cubes = [pot[pl.ds(at_ref[r, d] + 2 * CZB * l, CZB), :] for r in range(2)]
            out_ref[rows, l * LANES : (l + 1) * LANES] = jnp.concatenate(cubes, axis=0).astype(BF16)


def matrix_kernel(h, base, kinds, ret_ref, first, second, *rest):
    if h == 0:
        out_ref, acc, pot, perm, shuffled = rest
    else:
        other_ref, out_ref, acc, pot, perm, shuffled, vn = rest
    i = pl.program_id(0)
    pairs = BS // 2

    @pl.when(i == 0)
    def _():
        pot[...] = ret_ref[...].astype(F32)
        perm[...] = even_rows_first()
        acc[...] = jnp.zeros_like(acc)

    shuffled[...] = jnp.dot(
        perm[...], joined(first, second), preferred_element_type=F32
    ).astype(BF16)

    @pl.loop(0, NB // GROUP)
    def _(g):
        rows = pl.ds(pl.multiple_of(g * GROUP * BS, GROUP * BS), GROUP * BS)
        parts = []
        for t in range(GROUP):
            b = g * GROUP + t
            cells = [pot[pl.ds(base[b] + 2 * i + k, 1), :] for k in range(2)]
            cell = jnp.broadcast_to(jnp.concatenate(cells, axis=1), (BS, SEGW)).astype(BF16)
            parts.append(shuffled[pl.ds(pl.multiple_of(kinds[0, b] * BS, BS), BS), :] * cell)
        weighted = jnp.concatenate(parts, axis=0)
        acc[rows, :] = acc[rows, :] + lax.dot_general(
            weighted,
            joined(first, second),
            (((1,), (1,)), ((), ())),
            preferred_element_type=F32,
        )

    @pl.when(i == STEPS - 1)
    def _():
        low = lax.broadcasted_iota(jnp.int32, (pairs, LANES), 1) < BS

        @pl.loop(0, NB, unroll=4)
        def _(b):
            rows = pl.ds(pl.multiple_of(b * BS, BS), BS)
            kb = kinds[1, b]
            odd = (kb & 1) == 1
            v = jnp.where(kb < 2, acc[rows, 0:LANES], acc[rows, LANES : 2 * LANES])
            r = pltpu.roll(v, BS, 1)
            evens = jnp.where(odd, r[:pairs], v[:pairs])
            odds = jnp.where(odd, v[pairs:], r[pairs:])
            block = jnp.where(low, evens, odds)
            if h == 0:
                out_ref[b] = block
            else:
                vn[b] = block + other_ref[b]

        if h == 1:
            out_ref[...] = vn[...].reshape(NB, BS * BS).astype(BF16)


def make_tiles(h, small, density_blocks, basis):
    width = 2 * HALF + (LANES if h == 0 else 0)
    return pl.pallas_call(
        lambda *refs: tiles_kernel(h, *refs),
        grid=(STEPS,),
        in_specs=[SMEM] * 4 + [whole((NB, BS * BS))] + basis_specs(h),
        out_specs=[whole((DEVS * CZB, width)), SMEM],
        out_shape=[
            jax.ShapeDtypeStruct((DEVS * CZB, width), BF16),
            jax.ShapeDtypeStruct((NB,), jnp.int32),
        ],
        scratch_shapes=[
            pltpu.VMEM((NB, BS // 2, LANES), F32),
            pltpu.VMEM((NB * BS, KINDS * BS), BF16),
            pltpu.VMEM((KINDS * BS, SEGW), F32),
            pltpu.VMEM((KINDS * BS, KINDS * BS), BF16),
            pltpu.VMEM(((NB + 1) * CZB, HALF), F32),
            pltpu.SMEM((2 * DEVS,), jnp.int32),
        ],
        cost_estimate=cost(2 * NB * BS * KINDS * BS * CZB * HALF, 4 << 20),
    )(*small, density_blocks, basis, basis)


def gather_tiles(h, got, ext_potential, places=None):
    part = jax.ShapeDtypeStruct((CZB, PLANE // HALVES), F32)
    acc = pltpu.VMEM((SEGS * LPS * 2 * CZB, LANES), F32)
    if h == 0:
        return pl.pallas_call(
            gather_first,
            in_specs=[VMEM, VMEM],
            out_specs=[VMEM, VMEM, VMEM, SMEM],
            out_shape=[part, part, part, jax.ShapeDtypeStruct((8, DEVS), jnp.int32)],
            scratch_shapes=[
                pltpu.VMEM((DEVS * CZB, LANES), F32),
                pltpu.VMEM((8, DEVS), jnp.int32),
                acc,
                pltpu.SemaphoreType.DMA,
            ],
            cost_estimate=cost(1 << 20, 3 << 20),
            name="gather_tiles0",
        )(got, ext_potential)
    return pl.pallas_call(
        gather_second,
        in_specs=[SMEM, VMEM, VMEM],
        out_specs=[VMEM, VMEM, VMEM],
        out_shape=[part, part, part],
        scratch_shapes=[acc],
        cost_estimate=cost(1 << 20, 3 << 20),
        name="gather_tiles1",
    )(places, got, ext_potential)


def cut_cubes(h, places, own, rim, ext_potential, below, above, *other):
    width = PLANE // HALVES if h == 0 else PLANE
    return pl.pallas_call(
        lambda *refs: cubes_kernel(h, *refs),
        in_specs=[SMEM] + [VMEM] * (5 + len(other)),
        out_specs=[VMEM, VMEM],
        out_shape=[
            jax.ShapeDtypeStruct((CZB, width), F32),
            jax.ShapeDtypeStruct((DEVS * 16, HALF), BF16),
        ],
        scratch_shapes=[pltpu.VMEM((SEGS * LPS * 2 * CZB, LANES), F32)],
        cost_estimate=cost(1 << 20, 3 << 20),
    )(places, own, rim, ext_potential, below, above, *other)


def make_matrices(h, base, kinds, returned, basis, *other):
    blocks = (NB, BS // 2, LANES)
    out = (blocks, F32) if h == 0 else ((NB, BS * BS), BF16)
    return pl.pallas_call(
        lambda *refs: matrix_kernel(h, *refs),
        grid=(STEPS,),
        in_specs=[SMEM, SMEM, whole((DEVS * 16, HALF))]
        + basis_specs(h)
        + [whole(blocks)] * len(other),
        out_specs=whole(out[0]),
        out_shape=jax.ShapeDtypeStruct(*out),
        scratch_shapes=[
            pltpu.VMEM((NB * BS, KINDS * BS), F32),
            pltpu.VMEM((DEVS * 16, HALF), F32),
            pltpu.VMEM((KINDS * BS, KINDS * BS), BF16),
            pltpu.VMEM((KINDS * BS, SEGW), BF16),
        ]
        + [pltpu.VMEM(blocks, F32)] * h,
        cost_estimate=cost(2 * NB * BS * KINDS * BS * CZB * HALF, 4 << 20),
    )(base, kinds, returned, basis, basis, *other)


def shifted(x, by):
    return lax.ppermute(x, AXES, [(home(e), home((e + by) % DEVS)) for e in range(DEVS)])


def to_homes(x):
    return lax.ppermute(x, AXES, [(e, home(e)) for e in range(DEVS)])


def from_homes(x):
    return lax.ppermute(x, AXES, [(home(e), e) for e in range(DEVS)])


def exchanged(x):
    return lax.all_to_all(x, AXES, split_axis=0, concat_axis=0, tiled=True)


def local(
    density_blocks, block_owner, block_plane, block_segment, block_kinds, basis, ext_potential
):
    owner, kinds = block_owner.T, block_kinds.T
    ext_potential = to_homes(ext_potential)
    small = (owner, kinds, block_plane, block_segment)
    sent0, base = make_tiles(0, small, density_blocks, basis)
    sent1, _ = make_tiles(1, small, density_blocks, basis)
    got = [exchanged(sent0), exchanged(sent1)]

    own, rim, half, places = gather_tiles(0, got[0], ext_potential)
    below, above = shifted(rim, 1), shifted(half, -1)
    density, cubes = cut_cubes(0, places, own, rim, ext_potential, below, above)
    returned0 = exchanged(cubes)

    own, rim, half = gather_tiles(1, got[1], ext_potential, places)
    below, above = shifted(rim, 1), shifted(half, -1)
    density, cubes = cut_cubes(1, places, own, rim, ext_potential, below, above, density)
    returned1 = exchanged(cubes)
    density = from_homes(density)

    matrices = make_matrices(0, base, kinds, returned0, basis)
    matrices = make_matrices(1, base, kinds, returned1, basis, matrices)
    return density, matrices


def solution(mesh):
    rows = P(AXES, None)
    flat = P(AXES)
    return jax.shard_map(
        local,
        mesh=mesh,
        in_specs=(rows, rows, flat, flat, rows, P(), rows),
        out_specs=(rows, rows),
        check_vma=False,
    )
```

```python
import jax
import jax.numpy as jnp
from jax import lax
from jax.experimental import pallas as pl
from jax.experimental.pallas import tpu as pltpu
from jax.sharding import PartitionSpec as P


AXES = ("rows", "cols", "slab")
F32 = jnp.float32
BF16 = jnp.bfloat16
NB = 64
BS = 64
KINDS = 4
CZB = 8
SEGW = 512
SEGS = 8
DEVS = 128
PLANE = SEGS * SEGW
LANES = 128
CODE = 1024
HALVES = 2
HALF = SEGW // HALVES
LPS = HALF // LANES
STEPS = CZB // 2
GROUP = 64
TILES_MIB, SMALL_MIB, MATRICES_MIB = 63, 12, 62

SMEM = pl.BlockSpec(memory_space=pltpu.SMEM)
VMEM = pl.BlockSpec(memory_space=pltpu.VMEM)


def whole(shape):
    return pl.BlockSpec(shape, lambda i: (0,) * len(shape))


def basis_specs(h):
    def spec(t):
        return pl.BlockSpec((KINDS, BS, HALF), lambda i: (0, 0, (2 * i + t) * HALVES + h))

    return [spec(0), spec(1)]


def room(mib):
    return pltpu.CompilerParams(vmem_limit_bytes=mib << 20)


def cost(flops, moved):
    return pl.CostEstimate(flops=flops, bytes_accessed=moved, transcendentals=0)


def joined(first, second):
    parts = [ref[...].reshape(KINDS * BS, HALF) for ref in (first, second)]
    return jnp.concatenate(parts, axis=1)


def home(slab):
    chip = slab >> 1
    x, zi, yi = chip >> 4, (chip >> 2) & 3, chip & 3
    z = zi + (x & 1) * (3 - 2 * zi)
    y = yi + (zi & 1) * (3 - 2 * yi)
    return (x * 4 + z) * 8 + y * 2 + (slab & 1)


def first_slab(chip):
    x, z, y = chip >> 4, (chip >> 2) & 3, chip & 3
    zi = z + (x & 1) * (3 - 2 * z)
    yi = y + (zi & 1) * (3 - 2 * y)
    return 2 * (x * 16 + zi * 4 + yi)


def even_rows_first():
    shape = (KINDS * BS, KINDS * BS)
    to = lax.broadcasted_iota(jnp.int32, shape, 0)
    source = lax.broadcasted_iota(jnp.int32, shape, 1)
    row = to & (BS - 1)
    half = BS // 2
    wanted = (to - row) + jnp.where(row < half, 2 * row, 2 * (row - half) + 1)
    return jnp.where(source == wanted, 1.0, 0.0).astype(BF16)


def tiles_kernel(h, *refs):
    owner, kinds = refs[:2]
    if h == 0:
        plane, seg, dens_ref, first, second, out_ref = refs[2:8]
    else:
        dens_ref, first, second, out_ref, base = refs[2:7]
    pn, lhs, a32, perm, tiles, idx = refs[-6:]
    i = pl.program_id(0)
    pairs = BS // 2

    @pl.when(i == 0)
    def _():
        @pl.loop(0, 2 * DEVS, unroll=16)
        def _(o):
            idx[o] = NB * CZB

        @pl.loop(0, NB, unroll=4)
        def _(b):
            o = owner[0, b]
            was = idx[2 * o]
            after = idx[2 * o + 1]
            free = was == NB * CZB
            entry = b * CZB
            if h == 0:
                entry = entry + (plane[b] * SEGS + seg[b]) * CODE
            else:
                base[b] = home(o) * 16 + jnp.where(free, 0, CZB)
            idx[2 * o] = jnp.where(free, entry, was)
            idx[2 * o + 1] = jnp.where(free, after, entry)

        perm[...] = even_rows_first()
        pn[...] = dens_ref[...].astype(F32).reshape(NB, pairs, LANES)
        low = lax.broadcasted_iota(jnp.int32, (pairs, LANES), 1) < BS

        @pl.loop(0, NB, unroll=4)
        def _(b):
            rows = pl.ds(pl.multiple_of(b * BS, BS), BS)
            kb = kinds[1, b]
            odd = (kb & 1) == 1
            v = pn[b]
            r = pltpu.roll(v, BS, 1)
            keep = low != odd
            evens = jnp.where(keep, jnp.where(odd, r, v), 0.0)
            odds = jnp.where(keep, jnp.where(odd, v, r), 0.0)
            side = pl.multiple_of((kb >> 1) * LANES, LANES)
            lhs[rows, pl.ds(side, LANES)] = jnp.concatenate([evens, odds], axis=0).astype(BF16)
            lhs[rows, pl.ds(pl.multiple_of(LANES - side, LANES), LANES)] = jnp.zeros(
                (BS, LANES), BF16
            )

        tiles[pl.ds(NB * CZB, CZB), :] = jnp.zeros((CZB, HALF), F32)

    a32[...] = jnp.dot(perm[...], joined(first, second), preferred_element_type=F32)

    @pl.loop(0, NB // GROUP)
    def _(g):
        rows = pl.ds(pl.multiple_of(g * GROUP * BS, GROUP * BS), GROUP * BS)
        half = jnp.dot(lhs[rows, :], joined(first, second), preferred_element_type=F32)
        for t in range(GROUP):
            b = g * GROUP + t
            a = a32[pl.ds(pl.multiple_of(kinds[0, b] * BS, BS), BS), :]
            part = jnp.sum(a * half[t * BS : (t + 1) * BS], axis=0, keepdims=True)
            tiles[pl.ds(b * CZB + 2 * i, 1), :] = part[:, :HALF]
            tiles[pl.ds(b * CZB + 2 * i + 1, 1), :] = part[:, HALF:]

    @pl.when(i == STEPS - 1)
    def _():
        lane = lax.broadcasted_iota(jnp.int32, (CZB, LANES), 1)

        @pl.loop(0, DEVS // 2, unroll=4)
        def _(q):
            rows = pl.ds(pl.multiple_of(q * 16, 16), 16)
            slab = first_slab(q)
            slots = [idx[2 * slab + r] for r in range(4)]
            at = [pl.multiple_of(e & (CODE - 1), CZB) for e in slots]
            parts = [tiles[pl.ds(row, CZB), :] for row in at]
            out_ref[rows, 0:HALF] = jnp.concatenate([parts[0], parts[2]], axis=0).astype(BF16)
            out_ref[rows, HALF : 2 * HALF] = jnp.concatenate(
                [parts[1], parts[3]], axis=0
            ).astype(BF16)
            if h == 0:
                codes = [(e >> 10).astype(F32) for e in slots]
                marks = [
                    jnp.where(lane == 0, codes[2 * r], jnp.where(lane == 1, codes[2 * r + 1], 0.0))
                    for r in range(2)
                ]
                out_ref[rows, 2 * HALF :] = jnp.concatenate(marks, axis=0).astype(BF16)


def spread(at_ref, got_ref, ext_ref, own_ref, rim_ref, half_ref, acc, h):
    acc[...] = jnp.zeros_like(acc)

    @pl.loop(0, DEVS // 2, unroll=2)
    def _(q):
        rows = pl.ds(pl.multiple_of(q * 16, 16), 16)
        for r in range(2):
            both = got_ref[rows, r * HALF : (r + 1) * HALF].astype(F32)
            for t in range(2):
                row = at_ref[r, 2 * q + t]
                for l in range(LPS):
                    at = (pl.ds(row + 2 * CZB * l, CZB), slice(None))
                    acc[at] = acc[at] + both[t * CZB : (t + 1) * CZB, l * LANES : (l + 1) * LANES]

    for s in range(SEGS):
        for l in range(LPS):
            n = s * LPS + l
            cells = slice(n * LANES, (n + 1) * LANES)
            grid = slice(s * SEGW + h * HALF + l * LANES, s * SEGW + h * HALF + (l + 1) * LANES)
            row = 2 * CZB * n
            own = acc[row : row + CZB, :]
            own_ref[:, cells] = own
            rim_ref[:, cells] = acc[row + CZB : row + 2 * CZB, :]
            half_ref[:, cells] = ext_ref[:, grid] + 0.5 * own


def gather_first(got_ref, ext_ref, own_ref, rim_ref, half_ref, at_ref, marks, places, acc, sem):
    marks[...] = got_ref[:, 2 * HALF :].astype(F32)
    across = marks[pl.ds(0, DEVS, stride=CZB), :].T
    codes = across[0:2, :].astype(jnp.int32)
    places[0:2, :] = (codes >> 3) + (codes & 7) * (2 * CZB * LPS)
    copy = pltpu.make_async_copy(places, at_ref, sem)
    copy.start()
    copy.wait()
    spread(at_ref, got_ref, ext_ref, own_ref, rim_ref, half_ref, acc, 0)


def gather_second(at_ref, got_ref, ext_ref, own_ref, rim_ref, half_ref, acc):
    spread(at_ref, got_ref, ext_ref, own_ref, rim_ref, half_ref, acc, 1)


def cubes_kernel(h, at_ref, own_ref, rim_ref, ext_ref, below_ref, above_ref, *rest):
    if h == 0:
        dens_ref, out_ref, pot = rest
    else:
        other_ref, dens_ref, out_ref, pot = rest
    for s in range(SEGS):
        for l in range(LPS):
            n = s * LPS + l
            cells = slice(n * LANES, (n + 1) * LANES)
            grid = slice(s * SEGW + h * HALF + l * LANES, s * SEGW + h * HALF + (l + 1) * LANES)
            density = own_ref[:, cells] + below_ref[:, cells]
            if h == 0:
                dens_ref[:, cells] = density
            else:
                dens_ref[:, grid] = density
                dens_ref[:, s * SEGW + l * LANES : s * SEGW + (l + 1) * LANES] = other_ref[:, cells]
            row = 2 * CZB * n
            pot[row : row + CZB, :] = ext_ref[:, grid] + 0.5 * density
            pot[row + CZB : row + 2 * CZB, :] = above_ref[:, cells] + 0.5 * rim_ref[:, cells]

    @pl.loop(0, DEVS, unroll=4)
    def _(d):
        rows = pl.ds(pl.multiple_of(d * 16, 16), 16)
        for l in range(LPS):
            cubes = [pot[pl.ds(at_ref[r, d] + 2 * CZB * l, CZB), :] for r in range(2)]
            out_ref[rows, l * LANES : (l + 1) * LANES] = jnp.concatenate(cubes, axis=0).astype(BF16)


def matrix_kernel(h, base, kinds, ret_ref, first, second, *rest):
    if h == 0:
        out_ref, acc, pot, perm, shuffled = rest
    else:
        other_ref, dens_ref, out_ref, dens_out, acc, pot, perm, shuffled, vn = rest
    i = pl.program_id(0)
    pairs = BS // 2

    @pl.when(i == 0)
    def _():
        pot[...] = ret_ref[...].astype(F32)
        perm[...] = even_rows_first()

    shuffled[...] = jnp.dot(
        perm[...], joined(first, second), preferred_element_type=F32
    ).astype(BF16)

    @pl.loop(0, NB // GROUP)
    def _(g):
        rows = pl.ds(pl.multiple_of(g * GROUP * BS, GROUP * BS), GROUP * BS)
        parts = []
        for t in range(GROUP):
            b = g * GROUP + t
            cells = [pot[pl.ds(base[b] + 2 * i + k, 1), :] for k in range(2)]
            cell = jnp.broadcast_to(jnp.concatenate(cells, axis=1), (BS, SEGW)).astype(BF16)
            parts.append(shuffled[pl.ds(pl.multiple_of(kinds[0, b] * BS, BS), BS), :] * cell)
        weighted = jnp.concatenate(parts, axis=0)
        acc[rows, :] = jnp.where(i == 0, 0.0, acc[rows, :]) + lax.dot_general(
            weighted,
            joined(first, second),
            (((1,), (1,)), ((), ())),
            preferred_element_type=F32,
        )

    @pl.when(i == STEPS - 1)
    def _():
        low = lax.broadcasted_iota(jnp.int32, (pairs, LANES), 1) < BS

        @pl.loop(0, NB, unroll=4)
        def _(b):
            rows = pl.ds(pl.multiple_of(b * BS, BS), BS)
            kb = kinds[1, b]
            odd = (kb & 1) == 1
            v = jnp.where(kb < 2, acc[rows, 0:LANES], acc[rows, LANES : 2 * LANES])
            r = pltpu.roll(v, BS, 1)
            evens = jnp.where(odd, r[:pairs], v[:pairs])
            odds = jnp.where(odd, v[pairs:], r[pairs:])
            block = jnp.where(low, evens, odds)
            if h == 0:
                out_ref[b] = block
            else:
                vn[b] = block + other_ref[b]

        if h == 1:
            dens_out[...] = dens_ref[...]
            out_ref[...] = vn[...].reshape(NB, BS * BS).astype(BF16)


def make_tiles(h, small, density_blocks, basis):
    width = 2 * HALF + (LANES if h == 0 else 0)
    return pl.pallas_call(
        lambda *refs: tiles_kernel(h, *refs),
        grid=(STEPS,),
        in_specs=[SMEM] * len(small) + [whole((NB, BS * BS))] + basis_specs(h),
        out_specs=[whole((DEVS * CZB, width))] + [SMEM] * h,
        out_shape=[jax.ShapeDtypeStruct((DEVS * CZB, width), BF16)]
        + [jax.ShapeDtypeStruct((NB,), jnp.int32)] * h,
        scratch_shapes=[
            pltpu.VMEM((NB, BS // 2, LANES), F32),
            pltpu.VMEM((NB * BS, KINDS * BS), BF16),
            pltpu.VMEM((KINDS * BS, SEGW), F32),
            pltpu.VMEM((KINDS * BS, KINDS * BS), BF16),
            pltpu.VMEM(((NB + 1) * CZB, HALF), F32),
            pltpu.SMEM((2 * DEVS,), jnp.int32),
        ],
        cost_estimate=cost(2 * NB * BS * KINDS * BS * CZB * HALF, 4 << 20),
        compiler_params=room(TILES_MIB),
    )(*small, density_blocks, basis, basis)


def gather_tiles(h, got, ext_potential, places=None):
    part = jax.ShapeDtypeStruct((CZB, PLANE // HALVES), F32)
    acc = pltpu.VMEM((SEGS * LPS * 2 * CZB, LANES), F32)
    if h == 0:
        return pl.pallas_call(
            gather_first,
            in_specs=[VMEM, VMEM],
            out_specs=[VMEM, VMEM, VMEM, SMEM],
            out_shape=[part, part, part, jax.ShapeDtypeStruct((8, DEVS), jnp.int32)],
            scratch_shapes=[
                pltpu.VMEM((DEVS * CZB, LANES), F32),
                pltpu.VMEM((8, DEVS), jnp.int32),
                acc,
                pltpu.SemaphoreType.DMA,
            ],
            cost_estimate=cost(1 << 20, 3 << 20),
            compiler_params=room(SMALL_MIB),
            name="gather_tiles0",
        )(got, ext_potential)
    return pl.pallas_call(
        gather_second,
        in_specs=[SMEM, VMEM, VMEM],
        out_specs=[VMEM, VMEM, VMEM],
        out_shape=[part, part, part],
        scratch_shapes=[acc],
        cost_estimate=cost(1 << 20, 3 << 20),
        compiler_params=room(SMALL_MIB),
        name="gather_tiles1",
    )(places, got, ext_potential)


def cut_cubes(h, places, own, rim, ext_potential, below, above, *other):
    width = PLANE // HALVES if h == 0 else PLANE
    return pl.pallas_call(
        lambda *refs: cubes_kernel(h, *refs),
        in_specs=[SMEM] + [VMEM] * (5 + len(other)),
        out_specs=[VMEM, VMEM],
        out_shape=[
            jax.ShapeDtypeStruct((CZB, width), F32),
            jax.ShapeDtypeStruct((DEVS * 16, HALF), BF16),
        ],
        scratch_shapes=[pltpu.VMEM((SEGS * LPS * 2 * CZB, LANES), F32)],
        cost_estimate=cost(1 << 20, 3 << 20),
        compiler_params=room(SMALL_MIB),
    )(places, own, rim, ext_potential, below, above, *other)


def make_matrices(h, base, kinds, returned, basis, *other):
    blocks = (NB, BS // 2, LANES)
    out = (blocks, F32) if h == 0 else ((NB, BS * BS), BF16)
    return pl.pallas_call(
        lambda *refs: matrix_kernel(h, *refs),
        grid=(STEPS,),
        in_specs=[SMEM, SMEM, whole((DEVS * 16, HALF))]
        + basis_specs(h)
        + ([whole(blocks), whole((CZB, PLANE))] if h == 1 else []),
        out_specs=[whole(out[0])] + [whole((CZB, PLANE))] * h,
        out_shape=[jax.ShapeDtypeStruct(*out)] + [jax.ShapeDtypeStruct((CZB, PLANE), F32)] * h,
        scratch_shapes=[
            pltpu.VMEM((NB * BS, KINDS * BS), F32),
            pltpu.VMEM((DEVS * 16, HALF), F32),
            pltpu.VMEM((KINDS * BS, KINDS * BS), BF16),
            pltpu.VMEM((KINDS * BS, SEGW), BF16),
        ]
        + [pltpu.VMEM(blocks, F32)] * h,
        cost_estimate=cost(2 * NB * BS * KINDS * BS * CZB * HALF, 4 << 20),
        compiler_params=room(MATRICES_MIB),
    )(base, kinds, returned, basis, basis, *other)


def shifted(x, by):
    return lax.ppermute(x, AXES, [(home(e), home((e + by) % DEVS)) for e in range(DEVS)])


def to_homes(x):
    return lax.ppermute(x, AXES, [(e, home(e)) for e in range(DEVS)])


def from_homes(x):
    return lax.ppermute(x, AXES, [(home(e), e) for e in range(DEVS)])


def exchanged(x):
    return lax.all_to_all(x, AXES, split_axis=0, concat_axis=0, tiled=True)


def local(
    density_blocks, block_owner, block_plane, block_segment, block_kinds, basis, ext_potential
):
    owner, kinds = block_owner.T, block_kinds.T
    ext_potential = to_homes(ext_potential)
    small = (owner, kinds)
    (sent0,) = make_tiles(0, small + (block_plane, block_segment), density_blocks, basis)
    sent1, base = make_tiles(1, small, density_blocks, basis)
    got = [exchanged(sent0), exchanged(sent1)]

    own, rim, half, places = gather_tiles(0, got[0], ext_potential)
    below, above = shifted(rim, 1), shifted(half, -1)
    density, cubes = cut_cubes(0, places, own, rim, ext_potential, below, above)
    returned0 = exchanged(cubes)

    own, rim, half = gather_tiles(1, got[1], ext_potential, places)
    below, above = shifted(rim, 1), shifted(half, -1)
    density, cubes = cut_cubes(1, places, own, rim, ext_potential, below, above, density)
    returned1 = exchanged(cubes)
    density = from_homes(density)

    (partial,) = make_matrices(0, base, kinds, returned0, basis)
    matrices, density = make_matrices(1, base, kinds, returned1, basis, partial, density)
    return density, matrices


def solution(mesh):
    rows = P(AXES, None)
    flat = P(AXES)
    return jax.shard_map(
        local,
        mesh=mesh,
        in_specs=(rows, rows, flat, flat, rows, P(), rows),
        out_specs=(rows, rows),
        check_vma=False,
    )
```

```python
import jax
import jax.numpy as jnp
from jax import lax
from jax.experimental import pallas as pl
from jax.experimental.pallas import tpu as pltpu
from jax.sharding import PartitionSpec as P


AXES = ("rows", "cols", "slab")
F32 = jnp.float32
BF16 = jnp.bfloat16
NB = 64
BS = 64
KINDS = 4
CZB = 8
SEGW = 512
SEGS = 8
DEVS = 128
PLANE = SEGS * SEGW
LANES = 128
CODE = 1024
HALVES = 2
HALF = SEGW // HALVES
LPS = HALF // LANES
STEPS = CZB // 2
GROUP = 64
TILES_MIB, SMALL_MIB, MATRICES_MIB = 63, 12, 62

SMEM = pl.BlockSpec(memory_space=pltpu.SMEM)
VMEM = pl.BlockSpec(memory_space=pltpu.VMEM)


def whole(shape):
    return pl.BlockSpec(shape, lambda i: (0,) * len(shape))


def basis_specs(h):
    def spec(t):
        return pl.BlockSpec((KINDS, BS, HALF), lambda i: (0, 0, (2 * i + t) * HALVES + h))

    return [spec(0), spec(1)]


def room(mib):
    return pltpu.CompilerParams(vmem_limit_bytes=mib << 20)


def cost(flops, moved):
    return pl.CostEstimate(flops=flops, bytes_accessed=moved, transcendentals=0)


def joined(first, second):
    parts = [ref[...].reshape(KINDS * BS, HALF) for ref in (first, second)]
    return jnp.concatenate(parts, axis=1)


def home(slab):
    chip = slab >> 1
    x, zi, yi = chip >> 4, (chip >> 2) & 3, chip & 3
    z = zi + (x & 1) * (3 - 2 * zi)
    y = yi + (zi & 1) * (3 - 2 * yi)
    return (x * 4 + z) * 8 + y * 2 + (slab & 1)


def first_slab(chip):
    x, z, y = chip >> 4, (chip >> 2) & 3, chip & 3
    zi = z + (x & 1) * (3 - 2 * z)
    yi = y + (zi & 1) * (3 - 2 * y)
    return 2 * (x * 16 + zi * 4 + yi)


def even_rows_first():
    shape = (KINDS * BS, KINDS * BS)
    to = lax.broadcasted_iota(jnp.int32, shape, 0)
    source = lax.broadcasted_iota(jnp.int32, shape, 1)
    row = to & (BS - 1)
    half = BS // 2
    wanted = (to - row) + jnp.where(row < half, 2 * row, 2 * (row - half) + 1)
    return jnp.where(source == wanted, 1.0, 0.0).astype(BF16)


def tiles_kernel(h, *refs):
    owner, kinds = refs[:2]
    if h == 0:
        plane, seg, dens_ref, first, second, out_ref = refs[2:8]
    else:
        dens_ref, first, second, out_ref, base = refs[2:7]
    pn, lhs, a32, perm, tiles, idx = refs[-6:]
    i = pl.program_id(0)
    pairs = BS // 2

    @pl.when(i == 0)
    def _():
        @pl.loop(0, 2 * DEVS, unroll=16)
        def _(o):
            idx[o] = NB * CZB

        @pl.loop(0, NB, unroll=4)
        def _(b):
            o = owner[0, b]
            was = idx[2 * o]
            after = idx[2 * o + 1]
            free = was == NB * CZB
            entry = b * CZB
            if h == 0:
                entry = entry + (plane[b] * SEGS + seg[b]) * CODE
            else:
                base[b] = home(o) * 16 + jnp.where(free, 0, CZB)
            idx[2 * o] = jnp.where(free, entry, was)
            idx[2 * o + 1] = jnp.where(free, after, entry)

        perm[...] = even_rows_first()
        pn[...] = dens_ref[...].astype(F32).reshape(NB, pairs, LANES)
        low = lax.broadcasted_iota(jnp.int32, (pairs, LANES), 1) < BS

        @pl.loop(0, NB, unroll=4)
        def _(b):
            rows = pl.ds(pl.multiple_of(b * BS, BS), BS)
            kb = kinds[1, b]
            odd = (kb & 1) == 1
            v = pn[b]
            r = pltpu.roll(v, BS, 1)
            keep = low != odd
            evens = jnp.where(keep, jnp.where(odd, r, v), 0.0)
            odds = jnp.where(keep, jnp.where(odd, v, r), 0.0)
            side = pl.multiple_of((kb >> 1) * LANES, LANES)
            lhs[rows, pl.ds(side, LANES)] = jnp.concatenate([evens, odds], axis=0).astype(BF16)
            lhs[rows, pl.ds(pl.multiple_of(LANES - side, LANES), LANES)] = jnp.zeros(
                (BS, LANES), BF16
            )

        tiles[pl.ds(NB * CZB, CZB), :] = jnp.zeros((CZB, HALF), F32)

    a32[...] = jnp.dot(perm[...], joined(first, second), preferred_element_type=F32)

    @pl.loop(0, NB // GROUP)
    def _(g):
        rows = pl.ds(pl.multiple_of(g * GROUP * BS, GROUP * BS), GROUP * BS)
        half = jnp.dot(lhs[rows, :], joined(first, second), preferred_element_type=F32)
        for t in range(GROUP):
            b = g * GROUP + t
            a = a32[pl.ds(pl.multiple_of(kinds[0, b] * BS, BS), BS), :]
            part = jnp.sum(a * half[t * BS : (t + 1) * BS], axis=0, keepdims=True)
            tiles[pl.ds(b * CZB + 2 * i, 1), :] = part[:, :HALF]
            tiles[pl.ds(b * CZB + 2 * i + 1, 1), :] = part[:, HALF:]

    @pl.when(i == STEPS - 1)
    def _():
        lane = lax.broadcasted_iota(jnp.int32, (CZB, LANES), 1)

        @pl.loop(0, DEVS // 2, unroll=4)
        def _(q):
            rows = pl.ds(pl.multiple_of(q * 16, 16), 16)
            slab = first_slab(q)
            slots = [idx[2 * slab + r] for r in range(4)]
            at = [pl.multiple_of(e & (CODE - 1), CZB) for e in slots]
            parts = [tiles[pl.ds(row, CZB), :] for row in at]
            out_ref[rows, 0:HALF] = jnp.concatenate([parts[0], parts[2]], axis=0).astype(BF16)
            out_ref[rows, HALF : 2 * HALF] = jnp.concatenate(
                [parts[1], parts[3]], axis=0
            ).astype(BF16)
            if h == 0:
                codes = [(e >> 10).astype(F32) for e in slots]
                marks = [
                    jnp.where(lane == 0, codes[2 * r], jnp.where(lane == 1, codes[2 * r + 1], 0.0))
                    for r in range(2)
                ]
                out_ref[rows, 2 * HALF :] = jnp.concatenate(marks, axis=0).astype(BF16)


def spread(at_ref, got_ref, ext_ref, own_ref, rim_ref, near_ref, far_ref, acc, h):
    even = lax.axis_index("slab") == 0

    @pl.loop(0, DEVS // 2, unroll=2)
    def _(q):
        rows = pl.ds(pl.multiple_of(q * 16, 16), 16)
        for r in range(2):
            both = got_ref[rows, r * HALF : (r + 1) * HALF].astype(F32)
            for t in range(2):
                row = at_ref[r, 2 * q + t]
                for l in range(LPS):
                    at = (pl.ds(row + 2 * CZB * l, CZB), slice(None))
                    acc[at] = acc[at] + both[t * CZB : (t + 1) * CZB, l * LANES : (l + 1) * LANES]

    for s in range(SEGS):
        for l in range(LPS):
            n = s * LPS + l
            cells = slice(n * LANES, (n + 1) * LANES)
            grid = slice(s * SEGW + h * HALF + l * LANES, s * SEGW + h * HALF + (l + 1) * LANES)
            row = 2 * CZB * n
            own = acc[row : row + CZB, :]
            rim = acc[row + CZB : row + 2 * CZB, :]
            half = ext_ref[:, grid] + 0.5 * own
            own_ref[:, cells] = own
            rim_ref[:, cells] = rim
            near_ref[:, cells] = jnp.where(even, rim, half)
            far_ref[:, cells] = jnp.where(even, half, rim)


def gather_first(
    got_ref, ext_ref, own_ref, rim_ref, near_ref, far_ref, at_ref, marks, places, acc, sem
):
    marks[...] = got_ref[:, 2 * HALF :].astype(F32)
    across = marks[pl.ds(0, DEVS, stride=CZB), :].T
    codes = across[0:2, :].astype(jnp.int32)
    places[0:2, :] = (codes >> 3) + (codes & 7) * (2 * CZB * LPS)
    copy = pltpu.make_async_copy(places, at_ref, sem)
    copy.start()
    acc[...] = jnp.zeros_like(acc)
    copy.wait()
    spread(at_ref, got_ref, ext_ref, own_ref, rim_ref, near_ref, far_ref, acc, 0)


def gather_second(at_ref, got_ref, ext_ref, own_ref, rim_ref, near_ref, far_ref, acc):
    acc[...] = jnp.zeros_like(acc)
    spread(at_ref, got_ref, ext_ref, own_ref, rim_ref, near_ref, far_ref, acc, 1)


def cubes_kernel(h, at_ref, own_ref, rim_ref, ext_ref, near_ref, far_ref, *rest):
    if h == 0:
        dens_ref, out_ref, pot = rest
    else:
        other_ref, dens_ref, out_ref, pot = rest
    even = lax.axis_index("slab") == 0
    for s in range(SEGS):
        for l in range(LPS):
            n = s * LPS + l
            cells = slice(n * LANES, (n + 1) * LANES)
            grid = slice(s * SEGW + h * HALF + l * LANES, s * SEGW + h * HALF + (l + 1) * LANES)
            near, far = near_ref[:, cells], far_ref[:, cells]
            below = jnp.where(even, far, near)
            above = jnp.where(even, near, far)
            density = own_ref[:, cells] + below
            if h == 0:
                dens_ref[:, cells] = density
            else:
                dens_ref[:, grid] = density
                dens_ref[:, s * SEGW + l * LANES : s * SEGW + (l + 1) * LANES] = other_ref[:, cells]
            row = 2 * CZB * n
            pot[row : row + CZB, :] = ext_ref[:, grid] + 0.5 * density
            pot[row + CZB : row + 2 * CZB, :] = above + 0.5 * rim_ref[:, cells]

    @pl.loop(0, DEVS, unroll=4)
    def _(d):
        rows = pl.ds(pl.multiple_of(d * 16, 16), 16)
        for l in range(LPS):
            cubes = [pot[pl.ds(at_ref[r, d] + 2 * CZB * l, CZB), :] for r in range(2)]
            out_ref[rows, l * LANES : (l + 1) * LANES] = jnp.concatenate(cubes, axis=0).astype(BF16)


def matrix_kernel(h, base, kinds, ret_ref, first, second, *rest):
    if h == 0:
        out_ref, acc, pot, perm, shuffled = rest
    else:
        other_ref, out_ref, acc, pot, perm, shuffled, vn = rest
    i = pl.program_id(0)
    pairs = BS // 2

    @pl.when(i == 0)
    def _():
        pot[...] = ret_ref[...].astype(F32)
        perm[...] = even_rows_first()

    shuffled[...] = jnp.dot(
        perm[...], joined(first, second), preferred_element_type=F32
    ).astype(BF16)

    @pl.loop(0, NB // GROUP)
    def _(g):
        rows = pl.ds(pl.multiple_of(g * GROUP * BS, GROUP * BS), GROUP * BS)
        parts = []
        for t in range(GROUP):
            b = g * GROUP + t
            cells = [pot[pl.ds(base[b] + 2 * i + k, 1), :] for k in range(2)]
            cell = jnp.broadcast_to(jnp.concatenate(cells, axis=1), (BS, SEGW)).astype(BF16)
            parts.append(shuffled[pl.ds(pl.multiple_of(kinds[0, b] * BS, BS), BS), :] * cell)
        weighted = jnp.concatenate(parts, axis=0)
        acc[rows, :] = jnp.where(i == 0, 0.0, acc[rows, :]) + lax.dot_general(
            weighted,
            joined(first, second),
            (((1,), (1,)), ((), ())),
            preferred_element_type=F32,
        )

    @pl.when(i == STEPS - 1)
    def _():
        low = lax.broadcasted_iota(jnp.int32, (pairs, LANES), 1) < BS

        @pl.loop(0, NB, unroll=4)
        def _(b):
            rows = pl.ds(pl.multiple_of(b * BS, BS), BS)
            kb = kinds[1, b]
            odd = (kb & 1) == 1
            v = jnp.where(kb < 2, acc[rows, 0:LANES], acc[rows, LANES : 2 * LANES])
            r = pltpu.roll(v, BS, 1)
            evens = jnp.where(odd, r[:pairs], v[:pairs])
            odds = jnp.where(odd, v[pairs:], r[pairs:])
            block = jnp.where(low, evens, odds)
            if h == 0:
                out_ref[b] = block
            else:
                vn[b] = block + other_ref[b]

        if h == 1:
            out_ref[...] = vn[...].reshape(NB, BS * BS).astype(BF16)


def make_tiles(h, small, density_blocks, basis):
    width = 2 * HALF + (LANES if h == 0 else 0)
    return pl.pallas_call(
        lambda *refs: tiles_kernel(h, *refs),
        grid=(STEPS,),
        in_specs=[SMEM] * len(small) + [whole((NB, BS * BS))] + basis_specs(h),
        out_specs=[whole((DEVS * CZB, width))] + [SMEM] * h,
        out_shape=[jax.ShapeDtypeStruct((DEVS * CZB, width), BF16)]
        + [jax.ShapeDtypeStruct((NB,), jnp.int32)] * h,
        scratch_shapes=[
            pltpu.VMEM((NB, BS // 2, LANES), F32),
            pltpu.VMEM((NB * BS, KINDS * BS), BF16),
            pltpu.VMEM((KINDS * BS, SEGW), F32),
            pltpu.VMEM((KINDS * BS, KINDS * BS), BF16),
            pltpu.VMEM(((NB + 1) * CZB, HALF), F32),
            pltpu.SMEM((2 * DEVS,), jnp.int32),
        ],
        cost_estimate=cost(2 * NB * BS * KINDS * BS * CZB * HALF, 4 << 20),
        compiler_params=room(TILES_MIB),
    )(*small, density_blocks, basis, basis)


def gather_tiles(h, got, ext_potential, places=None):
    part = jax.ShapeDtypeStruct((CZB, PLANE // HALVES), F32)
    acc = pltpu.VMEM((SEGS * LPS * 2 * CZB, LANES), F32)
    if h == 0:
        return pl.pallas_call(
            gather_first,
            in_specs=[VMEM, VMEM],
            out_specs=[VMEM, VMEM, VMEM, VMEM, SMEM],
            out_shape=[part, part, part, part, jax.ShapeDtypeStruct((8, DEVS), jnp.int32)],
            scratch_shapes=[
                pltpu.VMEM((DEVS * CZB, LANES), F32),
                pltpu.VMEM((8, DEVS), jnp.int32),
                acc,
                pltpu.SemaphoreType.DMA,
            ],
            cost_estimate=cost(1 << 20, 3 << 20),
            compiler_params=room(SMALL_MIB),
            name="gather_tiles0",
        )(got, ext_potential)
    return pl.pallas_call(
        gather_second,
        in_specs=[SMEM, VMEM, VMEM],
        out_specs=[VMEM, VMEM, VMEM, VMEM],
        out_shape=[part, part, part, part],
        scratch_shapes=[acc],
        cost_estimate=cost(1 << 20, 3 << 20),
        compiler_params=room(SMALL_MIB),
        name="gather_tiles1",
    )(places, got, ext_potential)


def cut_cubes(h, places, own, rim, ext_potential, near, far, *other):
    width = PLANE // HALVES if h == 0 else PLANE
    return pl.pallas_call(
        lambda *refs: cubes_kernel(h, *refs),
        in_specs=[SMEM] + [VMEM] * (5 + len(other)),
        out_specs=[VMEM, VMEM],
        out_shape=[
            jax.ShapeDtypeStruct((CZB, width), F32),
            jax.ShapeDtypeStruct((DEVS * 16, HALF), BF16),
        ],
        scratch_shapes=[pltpu.VMEM((SEGS * LPS * 2 * CZB, LANES), F32)],
        cost_estimate=cost(1 << 20, 3 << 20),
        compiler_params=room(SMALL_MIB),
    )(places, own, rim, ext_potential, near, far, *other)


def make_matrices(h, base, kinds, returned, basis, *other):
    blocks = (NB, BS // 2, LANES)
    out = (blocks, F32) if h == 0 else ((NB, BS * BS), BF16)
    return pl.pallas_call(
        lambda *refs: matrix_kernel(h, *refs),
        grid=(STEPS,),
        in_specs=[SMEM, SMEM, whole((DEVS * 16, HALF))]
        + basis_specs(h)
        + [whole(blocks)] * h,
        out_specs=whole(out[0]),
        out_shape=jax.ShapeDtypeStruct(*out),
        scratch_shapes=[
            pltpu.VMEM((NB * BS, KINDS * BS), F32),
            pltpu.VMEM((DEVS * 16, HALF), F32),
            pltpu.VMEM((KINDS * BS, KINDS * BS), BF16),
            pltpu.VMEM((KINDS * BS, SEGW), BF16),
        ]
        + [pltpu.VMEM(blocks, F32)] * h,
        cost_estimate=cost(2 * NB * BS * KINDS * BS * CZB * HALF, 4 << 20),
        compiler_params=room(MATRICES_MIB),
    )(base, kinds, returned, basis, basis, *other)


def swapped(near, far):
    pairs = [(home(e), home(e ^ 1)) for e in range(DEVS)]
    next_pairs = [(home(e), home((((e + 1) ^ 1) - 1) % DEVS)) for e in range(DEVS)]
    return lax.ppermute(near, AXES, pairs), lax.ppermute(far, AXES, next_pairs)


def copy_kernel(in_ref, out_ref):
    out_ref[...] = in_ref[...]


def written(x):
    return pl.pallas_call(
        copy_kernel,
        in_specs=[VMEM],
        out_specs=VMEM,
        out_shape=jax.ShapeDtypeStruct(x.shape, x.dtype),
        compiler_params=room(SMALL_MIB),
        cost_estimate=cost(1 << 10, 1 << 18),
        name="written",
    )(x)


def to_homes(x):
    return lax.ppermute(x, AXES, [(e, home(e)) for e in range(DEVS)])


def from_homes(x):
    return lax.ppermute(x, AXES, [(home(e), e) for e in range(DEVS)])


def exchanged(x):
    return lax.all_to_all(x, AXES, split_axis=0, concat_axis=0, tiled=True)


def local(
    density_blocks, block_owner, block_plane, block_segment, block_kinds, basis, ext_potential
):
    owner, kinds = block_owner.T, block_kinds.T
    ext_potential = to_homes(ext_potential)
    small = (owner, kinds)
    (sent0,) = make_tiles(0, small + (block_plane, block_segment), density_blocks, basis)
    sent1, base = make_tiles(1, small, density_blocks, basis)
    got = [exchanged(sent0), exchanged(sent1)]

    own, rim, near, far, places = gather_tiles(0, got[0], ext_potential)
    near, far = swapped(near, far)
    density, cubes = cut_cubes(0, places, own, rim, ext_potential, near, far)
    returned0 = exchanged(cubes)

    own, rim, near, far = gather_tiles(1, got[1], ext_potential, places)
    near, far = swapped(near, far)
    density, cubes = cut_cubes(1, places, own, rim, ext_potential, near, far, density)
    returned1 = exchanged(cubes)
    density = from_homes(density)

    density = written(density)
    partial = make_matrices(0, base, kinds, returned0, basis)
    matrices = make_matrices(1, base, kinds, returned1, basis, partial)
    return density, matrices


def solution(mesh):
    rows = P(AXES, None)
    flat = P(AXES)
    return jax.shard_map(
        local,
        mesh=mesh,
        in_specs=(rows, rows, flat, flat, rows, P(), rows),
        out_specs=(rows, rows),
        check_vma=False,
    )
```

```python
import jax
import jax.numpy as jnp
from jax import lax
from jax.experimental import pallas as pl
from jax.experimental.pallas import tpu as pltpu
from jax.sharding import PartitionSpec as P


AXES = ("rows", "cols", "slab")
F32 = jnp.float32
BF16 = jnp.bfloat16
NB = 64
BS = 64
KINDS = 4
CZB = 8
SEGW = 512
SEGS = 8
DEVS = 128
PLANE = SEGS * SEGW
LANES = 128
CODE = 1024
HALVES = 2
HALF = SEGW // HALVES
LPS = HALF // LANES
STEPS = CZB // 2
GROUP = 64
TILES_MIB, SMALL_MIB, MATRICES_MIB = 63, 12, 62

SMEM = pl.BlockSpec(memory_space=pltpu.SMEM)
VMEM = pl.BlockSpec(memory_space=pltpu.VMEM)


def whole(shape):
    return pl.BlockSpec(shape, lambda i: (0,) * len(shape))


def basis_specs(h):
    def spec(t):
        return pl.BlockSpec((KINDS, BS, HALF), lambda i: (0, 0, (2 * i + t) * HALVES + h))

    return [spec(0), spec(1)]


def room(mib):
    return pltpu.CompilerParams(vmem_limit_bytes=mib << 20)


def moved_spec():
    return pl.BlockSpec((1, KINDS * BS, SEGW), lambda i: (i, 0, 0))


def cost(flops, moved):
    return pl.CostEstimate(flops=flops, bytes_accessed=moved, transcendentals=0)


def joined(first, second):
    parts = [ref[...].reshape(KINDS * BS, HALF) for ref in (first, second)]
    return jnp.concatenate(parts, axis=1)


def home(slab):
    chip = slab >> 1
    x, zi, yi = chip >> 4, (chip >> 2) & 3, chip & 3
    z = zi + (x & 1) * (3 - 2 * zi)
    y = yi + (zi & 1) * (3 - 2 * yi)
    return (x * 4 + z) * 8 + y * 2 + (slab & 1)


def even_rows_first():
    shape = (KINDS * BS, KINDS * BS)
    to = lax.broadcasted_iota(jnp.int32, shape, 0)
    source = lax.broadcasted_iota(jnp.int32, shape, 1)
    row = to & (BS - 1)
    half = BS // 2
    wanted = (to - row) + jnp.where(row < half, 2 * row, 2 * (row - half) + 1)
    return jnp.where(source == wanted, 1.0, 0.0).astype(BF16)


def tiles_kernel(h, *refs):
    owner, kinds = refs[:2]
    if h == 0:
        plane, seg, dens_ref, first, second, out_ref = refs[2:8]
    else:
        dens_ref, first, second, out_ref, base, moved_ref = refs[2:8]
    pn, lhs, a32, perm, tiles, idx = refs[-6:]
    i = pl.program_id(0)
    pairs = BS // 2

    @pl.when(i == 0)
    def _():
        @pl.loop(0, 2 * DEVS, unroll=16)
        def _(o):
            idx[o] = NB * CZB

        @pl.loop(0, NB, unroll=4)
        def _(b):
            o = owner[0, b]
            was = idx[2 * o]
            after = idx[2 * o + 1]
            free = was == NB * CZB
            entry = b * CZB
            if h == 0:
                entry = entry + (plane[b] * SEGS + seg[b]) * CODE
            else:
                base[b] = home(o) * 16 + jnp.where(free, 0, CZB)
            idx[2 * o] = jnp.where(free, entry, was)
            idx[2 * o + 1] = jnp.where(free, after, entry)

        perm[...] = even_rows_first()
        pn[...] = dens_ref[...].astype(F32).reshape(NB, pairs, LANES)
        low = lax.broadcasted_iota(jnp.int32, (pairs, LANES), 1) < BS

        @pl.loop(0, NB, unroll=4)
        def _(b):
            rows = pl.ds(pl.multiple_of(b * BS, BS), BS)
            kb = kinds[1, b]
            odd = (kb & 1) == 1
            v = pn[b]
            r = pltpu.roll(v, BS, 1)
            keep = low != odd
            evens = jnp.where(keep, jnp.where(odd, r, v), 0.0)
            odds = jnp.where(keep, jnp.where(odd, v, r), 0.0)
            side = pl.multiple_of((kb >> 1) * LANES, LANES)
            lhs[rows, pl.ds(side, LANES)] = jnp.concatenate([evens, odds], axis=0).astype(BF16)
            lhs[rows, pl.ds(pl.multiple_of(LANES - side, LANES), LANES)] = jnp.zeros(
                (BS, LANES), BF16
            )

        tiles[pl.ds(NB * CZB, CZB), :] = jnp.zeros((CZB, HALF), F32)

    a32[...] = jnp.dot(perm[...], joined(first, second), preferred_element_type=F32)
    if h == 1:
        moved_ref[0] = a32[...].astype(BF16)

    @pl.loop(0, NB // GROUP)
    def _(g):
        rows = pl.ds(pl.multiple_of(g * GROUP * BS, GROUP * BS), GROUP * BS)
        half = jnp.dot(lhs[rows, :], joined(first, second), preferred_element_type=F32)
        for t in range(GROUP):
            b = g * GROUP + t
            a = a32[pl.ds(pl.multiple_of(kinds[0, b] * BS, BS), BS), :]
            part = jnp.sum(a * half[t * BS : (t + 1) * BS], axis=0, keepdims=True)
            tiles[pl.ds(b * CZB + 2 * i, 1), :] = part[:, :HALF]
            tiles[pl.ds(b * CZB + 2 * i + 1, 1), :] = part[:, HALF:]

    @pl.when(i == STEPS - 1)
    def _():
        first_lane = lax.broadcasted_iota(jnp.int32, (CZB, LANES), 1) == 0

        @pl.loop(0, DEVS // 8)
        def _(g):
            x, z = g >> 2, g & 3
            zi = z + (x & 1) * (3 - 2 * z)
            row_slab = 8 * (x * 4 + zi)
            flip = zi & 1
            for y in range(4):
                rows = pl.ds(pl.multiple_of(g * 64, 64) + y * 16, 16)
                slot = 2 * (row_slab + 2 * (y + flip * (3 - 2 * y)))
                slots = [idx[slot + r] for r in range(4)]
                at = [pl.multiple_of(e & (CODE - 1), CZB) for e in slots]
                parts = [tiles[pl.ds(row, CZB), :] for row in at]
                out_ref[rows, 0:HALF] = jnp.concatenate([parts[0], parts[2]], axis=0).astype(BF16)
                out_ref[rows, HALF : 2 * HALF] = jnp.concatenate(
                    [parts[1], parts[3]], axis=0
                ).astype(BF16)
                if h == 0:
                    marks = [jnp.where(first_lane, slots[2 * r], slots[2 * r + 1]) for r in range(2)]
                    marks = (jnp.concatenate(marks, axis=0) >> 10).astype(F32)
                    out_ref[rows, 2 * HALF :] = marks.astype(BF16)


def spread(at_ref, got_ref, ext_ref, own_ref, rim_ref, near_ref, far_ref, acc, h):
    even = lax.axis_index("slab") == 0

    @pl.loop(0, DEVS // 2, unroll=2)
    def _(q):
        rows = pl.ds(pl.multiple_of(q * 16, 16), 16)
        for r in range(2):
            both = got_ref[rows, r * HALF : (r + 1) * HALF].astype(F32)
            for t in range(2):
                row = at_ref[r, 2 * q + t]
                for l in range(LPS):
                    at = (pl.ds(row + 2 * CZB * l, CZB), slice(None))
                    acc[at] = acc[at] + both[t * CZB : (t + 1) * CZB, l * LANES : (l + 1) * LANES]

    for s in range(SEGS):
        for l in range(LPS):
            n = s * LPS + l
            cells = slice(n * LANES, (n + 1) * LANES)
            grid = slice(s * SEGW + h * HALF + l * LANES, s * SEGW + h * HALF + (l + 1) * LANES)
            row = 2 * CZB * n
            own = acc[row : row + CZB, :]
            rim = acc[row + CZB : row + 2 * CZB, :]
            half = ext_ref[:, grid] + 0.5 * own
            own_ref[:, cells] = own
            rim_ref[:, cells] = rim
            near_ref[:, cells] = jnp.where(even, rim, half)
            far_ref[:, cells] = jnp.where(even, half, rim)


def gather_first(
    got_ref, ext_ref, own_ref, rim_ref, near_ref, far_ref, at_ref, marks, places, acc, sem
):
    marks[...] = got_ref[:, 2 * HALF :].astype(F32)
    across = marks[pl.ds(0, DEVS, stride=CZB), :].T
    codes = across[0:2, :].astype(jnp.int32)
    places[0:2, :] = (codes >> 3) + (codes & 7) * (2 * CZB * LPS)
    copy = pltpu.make_async_copy(places, at_ref, sem)
    copy.start()
    acc[...] = jnp.zeros_like(acc)
    copy.wait()
    spread(at_ref, got_ref, ext_ref, own_ref, rim_ref, near_ref, far_ref, acc, 0)


def gather_second(at_ref, got_ref, ext_ref, own_ref, rim_ref, near_ref, far_ref, acc):
    acc[...] = jnp.zeros_like(acc)
    spread(at_ref, got_ref, ext_ref, own_ref, rim_ref, near_ref, far_ref, acc, 1)


def cubes_kernel(h, at_ref, own_ref, rim_ref, ext_ref, near_ref, far_ref, *rest):
    if h == 0:
        dens_ref, out_ref, pot = rest
    else:
        other_ref, dens_ref, out_ref, pot = rest
    even = lax.axis_index("slab") == 0
    for s in range(SEGS):
        for l in range(LPS):
            n = s * LPS + l
            cells = slice(n * LANES, (n + 1) * LANES)
            grid = slice(s * SEGW + h * HALF + l * LANES, s * SEGW + h * HALF + (l + 1) * LANES)
            near, far = near_ref[:, cells], far_ref[:, cells]
            below = jnp.where(even, far, near)
            above = jnp.where(even, near, far)
            density = own_ref[:, cells] + below
            if h == 0:
                dens_ref[:, cells] = density
            else:
                dens_ref[:, grid] = density
                dens_ref[:, s * SEGW + l * LANES : s * SEGW + (l + 1) * LANES] = other_ref[:, cells]
            row = 2 * CZB * n
            pot[row : row + CZB, :] = ext_ref[:, grid] + 0.5 * density
            pot[row + CZB : row + 2 * CZB, :] = above + 0.5 * rim_ref[:, cells]

    @pl.loop(0, DEVS, unroll=4)
    def _(d):
        rows = pl.ds(pl.multiple_of(d * 16, 16), 16)
        for l in range(LPS):
            cubes = [pot[pl.ds(at_ref[r, d] + 2 * CZB * l, CZB), :] for r in range(2)]
            out_ref[rows, l * LANES : (l + 1) * LANES] = jnp.concatenate(cubes, axis=0).astype(BF16)


def matrix_kernel(h, base, kinds, ret_ref, first, second, *rest):
    if h == 0:
        out_ref, acc, pot, perm, shuffled = rest
    else:
        other_ref, moved, out_ref, acc, pot, vn = rest
        shuffled = moved.at[0]
    i = pl.program_id(0)
    pairs = BS // 2

    @pl.when(i == 0)
    def _():
        pot[...] = ret_ref[...].astype(F32)
        if h == 0:
            perm[...] = even_rows_first()

    if h == 0:
        shuffled[...] = jnp.dot(
            perm[...], joined(first, second), preferred_element_type=F32
        ).astype(BF16)

    @pl.loop(0, NB // GROUP)
    def _(g):
        rows = pl.ds(pl.multiple_of(g * GROUP * BS, GROUP * BS), GROUP * BS)
        parts = []
        for t in range(GROUP):
            b = g * GROUP + t
            cells = [pot[pl.ds(base[b] + 2 * i + k, 1), :] for k in range(2)]
            cell = jnp.broadcast_to(jnp.concatenate(cells, axis=1), (BS, SEGW)).astype(BF16)
            parts.append(shuffled[pl.ds(pl.multiple_of(kinds[0, b] * BS, BS), BS), :] * cell)
        weighted = jnp.concatenate(parts, axis=0)
        acc[rows, :] = jnp.where(i == 0, 0.0, acc[rows, :]) + lax.dot_general(
            weighted,
            joined(first, second),
            (((1,), (1,)), ((), ())),
            preferred_element_type=F32,
        )

    @pl.when(i == STEPS - 1)
    def _():
        low = lax.broadcasted_iota(jnp.int32, (pairs, LANES), 1) < BS

        @pl.loop(0, NB, unroll=4)
        def _(b):
            rows = pl.ds(pl.multiple_of(b * BS, BS), BS)
            kb = kinds[1, b]
            odd = (kb & 1) == 1
            v = jnp.where(kb < 2, acc[rows, 0:LANES], acc[rows, LANES : 2 * LANES])
            r = pltpu.roll(v, BS, 1)
            evens = jnp.where(odd, r[:pairs], v[:pairs])
            odds = jnp.where(odd, v[pairs:], r[pairs:])
            block = jnp.where(low, evens, odds)
            if h == 0:
                out_ref[b] = block
            else:
                vn[b] = block + other_ref[b]

        if h == 1:
            out_ref[...] = vn[...].reshape(NB, BS * BS).astype(BF16)


def make_tiles(h, small, density_blocks, basis):
    width = 2 * HALF + (LANES if h == 0 else 0)
    return pl.pallas_call(
        lambda *refs: tiles_kernel(h, *refs),
        grid=(STEPS,),
        in_specs=[SMEM] * len(small) + [whole((NB, BS * BS))] + basis_specs(h),
        out_specs=[whole((DEVS * CZB, width))] + [SMEM, moved_spec()] * h,
        out_shape=[jax.ShapeDtypeStruct((DEVS * CZB, width), BF16)]
        + [
            jax.ShapeDtypeStruct((NB,), jnp.int32),
            jax.ShapeDtypeStruct((STEPS, KINDS * BS, SEGW), BF16),
        ]
        * h,
        scratch_shapes=[
            pltpu.VMEM((NB, BS // 2, LANES), F32),
            pltpu.VMEM((NB * BS, KINDS * BS), BF16),
            pltpu.VMEM((KINDS * BS, SEGW), F32),
            pltpu.VMEM((KINDS * BS, KINDS * BS), BF16),
            pltpu.VMEM(((NB + 1) * CZB, HALF), F32),
            pltpu.SMEM((2 * DEVS,), jnp.int32),
        ],
        cost_estimate=cost(2 * NB * BS * KINDS * BS * CZB * HALF, 4 << 20),
        compiler_params=room(TILES_MIB),
    )(*small, density_blocks, basis, basis)


def gather_tiles(h, got, ext_potential, places=None):
    part = jax.ShapeDtypeStruct((CZB, PLANE // HALVES), F32)
    acc = pltpu.VMEM((SEGS * LPS * 2 * CZB, LANES), F32)
    if h == 0:
        return pl.pallas_call(
            gather_first,
            in_specs=[VMEM, VMEM],
            out_specs=[VMEM, VMEM, VMEM, VMEM, SMEM],
            out_shape=[part, part, part, part, jax.ShapeDtypeStruct((8, DEVS), jnp.int32)],
            scratch_shapes=[
                pltpu.VMEM((DEVS * CZB, LANES), F32),
                pltpu.VMEM((8, DEVS), jnp.int32),
                acc,
                pltpu.SemaphoreType.DMA,
            ],
            cost_estimate=cost(1 << 20, 3 << 20),
            compiler_params=room(SMALL_MIB),
            name="gather_tiles0",
        )(got, ext_potential)
    return pl.pallas_call(
        gather_second,
        in_specs=[SMEM, VMEM, VMEM],
        out_specs=[VMEM, VMEM, VMEM, VMEM],
        out_shape=[part, part, part, part],
        scratch_shapes=[acc],
        cost_estimate=cost(1 << 20, 3 << 20),
        compiler_params=room(SMALL_MIB),
        name="gather_tiles1",
    )(places, got, ext_potential)


def cut_cubes(h, places, own, rim, ext_potential, near, far, *other):
    width = PLANE // HALVES if h == 0 else PLANE
    return pl.pallas_call(
        lambda *refs: cubes_kernel(h, *refs),
        in_specs=[SMEM] + [VMEM] * (5 + len(other)),
        out_specs=[VMEM, VMEM],
        out_shape=[
            jax.ShapeDtypeStruct((CZB, width), F32),
            jax.ShapeDtypeStruct((DEVS * 16, HALF), BF16),
        ],
        scratch_shapes=[pltpu.VMEM((SEGS * LPS * 2 * CZB, LANES), F32)],
        cost_estimate=cost(1 << 20, 3 << 20),
        compiler_params=room(SMALL_MIB),
    )(places, own, rim, ext_potential, near, far, *other)


def make_matrices(h, base, kinds, returned, basis, *other):
    blocks = (NB, BS // 2, LANES)
    out = (blocks, F32) if h == 0 else ((NB, BS * BS), BF16)
    return pl.pallas_call(
        lambda *refs: matrix_kernel(h, *refs),
        grid=(STEPS,),
        in_specs=[SMEM, SMEM, whole((DEVS * 16, HALF))]
        + basis_specs(h)
        + [whole(blocks), moved_spec()] * h,
        out_specs=whole(out[0]),
        out_shape=jax.ShapeDtypeStruct(*out),
        scratch_shapes=[
            pltpu.VMEM((NB * BS, KINDS * BS), F32),
            pltpu.VMEM((DEVS * 16, HALF), F32),
        ]
        + [
            pltpu.VMEM((KINDS * BS, KINDS * BS), BF16),
            pltpu.VMEM((KINDS * BS, SEGW), BF16),
        ]
        * (1 - h)
        + [pltpu.VMEM(blocks, F32)] * h,
        cost_estimate=cost(2 * NB * BS * KINDS * BS * CZB * HALF, 4 << 20),
        compiler_params=room(MATRICES_MIB),
    )(base, kinds, returned, basis, basis, *other)


def swapped(near, far):
    pairs = [(home(e), home(e ^ 1)) for e in range(DEVS)]
    next_pairs = [(home(e), home((((e + 1) ^ 1) - 1) % DEVS)) for e in range(DEVS)]
    return lax.ppermute(near, AXES, pairs), lax.ppermute(far, AXES, next_pairs)


def copy_kernel(in_ref, out_ref):
    out_ref[...] = in_ref[...]


def written(x):
    return pl.pallas_call(
        copy_kernel,
        in_specs=[VMEM],
        out_specs=VMEM,
        out_shape=jax.ShapeDtypeStruct(x.shape, x.dtype),
        compiler_params=room(SMALL_MIB),
        cost_estimate=cost(1 << 10, 1 << 18),
        name="written",
    )(x)


def to_homes(x):
    return lax.ppermute(x, AXES, [(e, home(e)) for e in range(DEVS)])


def from_homes(x):
    return lax.ppermute(x, AXES, [(home(e), e) for e in range(DEVS)])


def exchanged(x):
    return lax.all_to_all(x, AXES, split_axis=0, concat_axis=0, tiled=True)


def local(
    density_blocks, block_owner, block_plane, block_segment, block_kinds, basis, ext_potential
):
    owner, kinds = block_owner.T, block_kinds.T
    ext_potential = to_homes(ext_potential)
    small = (owner, kinds)
    (sent0,) = make_tiles(0, small + (block_plane, block_segment), density_blocks, basis)
    sent1, base, moved = make_tiles(1, small, density_blocks, basis)
    got = [exchanged(sent0), exchanged(sent1)]

    own, rim, near, far, places = gather_tiles(0, got[0], ext_potential)
    near, far = swapped(near, far)
    density, cubes = cut_cubes(0, places, own, rim, ext_potential, near, far)
    returned0 = exchanged(cubes)

    own, rim, near, far = gather_tiles(1, got[1], ext_potential, places)
    near, far = swapped(near, far)
    density, cubes = cut_cubes(1, places, own, rim, ext_potential, near, far, density)
    returned1 = exchanged(cubes)
    density = from_homes(density)

    density = written(density)
    partial = make_matrices(0, base, kinds, returned0, basis)
    matrices = make_matrices(1, base, kinds, returned1, basis, partial, moved)
    return density, matrices


def solution(mesh):
    rows = P(AXES, None)
    flat = P(AXES)
    return jax.shard_map(
        local,
        mesh=mesh,
        in_specs=(rows, rows, flat, flat, rows, P(), rows),
        out_specs=(rows, rows),
        check_vma=False,
    )
```

```python
import jax
import jax.numpy as jnp
from jax import lax
from jax.experimental import pallas as pl
from jax.experimental.pallas import tpu as pltpu
from jax.sharding import PartitionSpec as P


AXES = ("rows", "cols", "slab")
F32 = jnp.float32
BF16 = jnp.bfloat16
NB = 64
BS = 64
KINDS = 4
CZB = 8
SEGW = 512
SEGS = 8
DEVS = 128
PLANE = SEGS * SEGW
LANES = 128
CODE = 1024
HALVES = 2
HALF = SEGW // HALVES
LPS = HALF // LANES
STEPS = CZB // 2
GROUP = 64
TILES_MIB, SMALL_MIB, MATRICES_MIB = 63, 12, 62

SMEM = pl.BlockSpec(memory_space=pltpu.SMEM)
VMEM = pl.BlockSpec(memory_space=pltpu.VMEM)


def whole(shape):
    return pl.BlockSpec(shape, lambda i: (0,) * len(shape))


def basis_specs(h):
    def spec(t):
        return pl.BlockSpec((KINDS, BS, HALF), lambda i: (0, 0, (2 * i + t) * HALVES + h))

    return [spec(0), spec(1)]


def room(mib):
    return pltpu.CompilerParams(vmem_limit_bytes=mib << 20)


def moved_spec():
    return pl.BlockSpec((1, KINDS * BS, SEGW), lambda i: (i, 0, 0))


def cost(flops, moved):
    return pl.CostEstimate(flops=flops, bytes_accessed=moved, transcendentals=0)


def joined(first, second):
    parts = [ref[...].reshape(KINDS * BS, HALF) for ref in (first, second)]
    return jnp.concatenate(parts, axis=1)


def home(slab):
    chip = slab >> 1
    x, zi, yi = chip >> 4, (chip >> 2) & 3, chip & 3
    z = zi + (x & 1) * (3 - 2 * zi)
    y = yi + (zi & 1) * (3 - 2 * yi)
    return (x * 4 + z) * 8 + y * 2 + (slab & 1)


def even_rows_first():
    shape = (KINDS * BS, KINDS * BS)
    to = lax.broadcasted_iota(jnp.int32, shape, 0)
    source = lax.broadcasted_iota(jnp.int32, shape, 1)
    row = to & (BS - 1)
    half = BS // 2
    wanted = (to - row) + jnp.where(row < half, 2 * row, 2 * (row - half) + 1)
    return jnp.where(source == wanted, 1.0, 0.0).astype(BF16)


def tiles_kernel(h, *refs):
    owner, kinds = refs[:2]
    if h == 0:
        plane, seg, dens_ref, first, second, out_ref = refs[2:8]
    else:
        dens_ref, first, second, out_ref, base, moved_ref = refs[2:8]
    pn, lhs, a32, perm, tiles, idx = refs[-6:]
    i = pl.program_id(0)
    pairs = BS // 2

    @pl.when(i == 0)
    def _():
        @pl.loop(0, 2 * DEVS, unroll=16)
        def _(o):
            idx[o] = NB * CZB

        @pl.loop(0, NB, unroll=4)
        def _(b):
            o = owner[0, b]
            was = idx[2 * o]
            after = idx[2 * o + 1]
            free = was == NB * CZB
            entry = b * CZB
            if h == 0:
                entry = entry + (plane[b] * SEGS + seg[b]) * CODE
            else:
                base[b] = home(o) * 16 + jnp.where(free, 0, CZB)
            idx[2 * o] = jnp.where(free, entry, was)
            idx[2 * o + 1] = jnp.where(free, after, entry)

        perm[...] = even_rows_first()
        pn[...] = dens_ref[...].astype(F32).reshape(NB, pairs, LANES)
        low = lax.broadcasted_iota(jnp.int32, (pairs, LANES), 1) < BS

        @pl.loop(0, NB, unroll=4)
        def _(b):
            rows = pl.ds(pl.multiple_of(b * BS, BS), BS)
            kb = kinds[1, b]
            odd = (kb & 1) == 1
            v = pn[b]
            r = pltpu.roll(v, BS, 1)
            keep = low != odd
            evens = jnp.where(keep, jnp.where(odd, r, v), 0.0)
            odds = jnp.where(keep, jnp.where(odd, v, r), 0.0)
            side = pl.multiple_of((kb >> 1) * LANES, LANES)
            lhs[rows, pl.ds(side, LANES)] = jnp.concatenate([evens, odds], axis=0).astype(BF16)
            lhs[rows, pl.ds(pl.multiple_of(LANES - side, LANES), LANES)] = jnp.zeros(
                (BS, LANES), BF16
            )

        tiles[pl.ds(NB * CZB, CZB), :] = jnp.zeros((CZB, HALF), F32)

    a32[...] = jnp.dot(perm[...], joined(first, second), preferred_element_type=F32)
    if h == 1:
        moved_ref[0] = a32[...].astype(BF16)

    @pl.loop(0, NB // GROUP)
    def _(g):
        rows = pl.ds(pl.multiple_of(g * GROUP * BS, GROUP * BS), GROUP * BS)
        half = jnp.dot(lhs[rows, :], joined(first, second), preferred_element_type=F32)
        for t in range(GROUP):
            b = g * GROUP + t
            a = a32[pl.ds(pl.multiple_of(kinds[0, b] * BS, BS), BS), :]
            part = jnp.sum(a * half[t * BS : (t + 1) * BS], axis=0, keepdims=True)
            tiles[pl.ds(b * CZB + 2 * i, 1), :] = part[:, :HALF]
            tiles[pl.ds(b * CZB + 2 * i + 1, 1), :] = part[:, HALF:]

    @pl.when(i == STEPS - 1)
    def _():
        first_lane = lax.broadcasted_iota(jnp.int32, (CZB, LANES), 1) == 0

        @pl.loop(0, DEVS // 8)
        def _(g):
            x, z = g >> 2, g & 3
            zi = z + (x & 1) * (3 - 2 * z)
            row_slab = 8 * (x * 4 + zi)
            flip = zi & 1
            for y in range(4):
                rows = pl.ds(pl.multiple_of(g * 64, 64) + y * 16, 16)
                slot = 2 * (row_slab + 2 * (y + flip * (3 - 2 * y)))
                slots = [idx[slot + r] for r in range(4)]
                at = [pl.multiple_of(e & (CODE - 1), CZB) for e in slots]
                parts = [tiles[pl.ds(row, CZB), :] for row in at]
                out_ref[rows, 0:HALF] = jnp.concatenate([parts[0], parts[2]], axis=0).astype(BF16)
                out_ref[rows, HALF : 2 * HALF] = jnp.concatenate(
                    [parts[1], parts[3]], axis=0
                ).astype(BF16)
                if h == 0:
                    marks = [jnp.where(first_lane, slots[2 * r], slots[2 * r + 1]) for r in range(2)]
                    marks = (jnp.concatenate(marks, axis=0) >> 10).astype(F32)
                    out_ref[rows, 2 * HALF :] = marks.astype(BF16)


def spread(at_ref, got_ref, ext_ref, own_ref, rim_ref, near_ref, far_ref, acc, h):
    even = lax.axis_index("slab") == 0

    @pl.loop(0, DEVS // 2, unroll=8)
    def _(q):
        rows = pl.ds(pl.multiple_of(q * 16, 16), 16)
        for r in range(2):
            both = got_ref[rows, r * HALF : (r + 1) * HALF].astype(F32)
            for t in range(2):
                row = at_ref[r, 2 * q + t]
                for l in range(LPS):
                    at = (pl.ds(row + 2 * CZB * l, CZB), slice(None))
                    acc[at] = acc[at] + both[t * CZB : (t + 1) * CZB, l * LANES : (l + 1) * LANES]

    for s in range(SEGS):
        for l in range(LPS):
            n = s * LPS + l
            cells = slice(n * LANES, (n + 1) * LANES)
            grid = slice(s * SEGW + h * HALF + l * LANES, s * SEGW + h * HALF + (l + 1) * LANES)
            row = 2 * CZB * n
            own = acc[row : row + CZB, :]
            rim = acc[row + CZB : row + 2 * CZB, :]
            half = ext_ref[:, grid] + 0.5 * own
            own_ref[:, cells] = own
            rim_ref[:, cells] = rim
            near_ref[:, cells] = jnp.where(even, rim, half).astype(BF16)
            far_ref[:, cells] = jnp.where(even, half, rim).astype(BF16)


def gather_first(
    got_ref, ext_ref, own_ref, rim_ref, near_ref, far_ref, at_ref, marks, places, acc, sem
):
    marks[...] = got_ref[:, 2 * HALF :].astype(F32)
    across = marks[pl.ds(0, DEVS, stride=CZB), :].T
    codes = across[0:2, :].astype(jnp.int32)
    places[0:2, :] = (codes >> 3) + (codes & 7) * (2 * CZB * LPS)
    copy = pltpu.make_async_copy(places, at_ref, sem)
    copy.start()
    acc[...] = jnp.zeros_like(acc)
    copy.wait()
    spread(at_ref, got_ref, ext_ref, own_ref, rim_ref, near_ref, far_ref, acc, 0)


def gather_second(at_ref, got_ref, ext_ref, own_ref, rim_ref, near_ref, far_ref, acc):
    acc[...] = jnp.zeros_like(acc)
    spread(at_ref, got_ref, ext_ref, own_ref, rim_ref, near_ref, far_ref, acc, 1)


def cubes_kernel(h, at_ref, own_ref, rim_ref, ext_ref, near_ref, far_ref, *rest):
    if h == 0:
        dens_ref, out_ref, pot = rest
    else:
        other_ref, dens_ref, out_ref, pot = rest
    even = lax.axis_index("slab") == 0
    for s in range(SEGS):
        for l in range(LPS):
            n = s * LPS + l
            cells = slice(n * LANES, (n + 1) * LANES)
            grid = slice(s * SEGW + h * HALF + l * LANES, s * SEGW + h * HALF + (l + 1) * LANES)
            near, far = near_ref[:, cells].astype(F32), far_ref[:, cells].astype(F32)
            below = jnp.where(even, far, near)
            above = jnp.where(even, near, far)
            density = own_ref[:, cells] + below
            if h == 0:
                dens_ref[:, cells] = density
            else:
                dens_ref[:, grid] = density
                dens_ref[:, s * SEGW + l * LANES : s * SEGW + (l + 1) * LANES] = other_ref[:, cells]
            row = 2 * CZB * n
            pot[row : row + CZB, :] = ext_ref[:, grid] + 0.5 * density
            pot[row + CZB : row + 2 * CZB, :] = above + 0.5 * rim_ref[:, cells]

    @pl.loop(0, DEVS, unroll=16)
    def _(d):
        rows = pl.ds(pl.multiple_of(d * 16, 16), 16)
        for l in range(LPS):
            cubes = [pot[pl.ds(at_ref[r, d] + 2 * CZB * l, CZB), :] for r in range(2)]
            out_ref[rows, l * LANES : (l + 1) * LANES] = jnp.concatenate(cubes, axis=0).astype(BF16)


def matrix_kernel(h, base, kinds, ret_ref, first, second, *rest):
    if h == 0:
        out_ref, acc, pot, perm, shuffled = rest
    else:
        other_ref, moved, out_ref, acc, pot, vn = rest
        shuffled = moved.at[0]
    i = pl.program_id(0)
    pairs = BS // 2

    @pl.when(i == 0)
    def _():
        pot[...] = ret_ref[...].astype(F32)
        if h == 0:
            perm[...] = even_rows_first()

    if h == 0:
        shuffled[...] = jnp.dot(
            perm[...], joined(first, second), preferred_element_type=F32
        ).astype(BF16)

    @pl.loop(0, NB // GROUP)
    def _(g):
        rows = pl.ds(pl.multiple_of(g * GROUP * BS, GROUP * BS), GROUP * BS)
        parts = []
        for t in range(GROUP):
            b = g * GROUP + t
            cells = [pot[pl.ds(base[b] + 2 * i + k, 1), :] for k in range(2)]
            cell = jnp.broadcast_to(jnp.concatenate(cells, axis=1), (BS, SEGW)).astype(BF16)
            parts.append(shuffled[pl.ds(pl.multiple_of(kinds[0, b] * BS, BS), BS), :] * cell)
        weighted = jnp.concatenate(parts, axis=0)
        acc[rows, :] = jnp.where(i == 0, 0.0, acc[rows, :]) + lax.dot_general(
            weighted,
            joined(first, second),
            (((1,), (1,)), ((), ())),
            preferred_element_type=F32,
        )

    @pl.when(i == STEPS - 1)
    def _():
        low = lax.broadcasted_iota(jnp.int32, (pairs, LANES), 1) < BS

        @pl.loop(0, NB, unroll=4)
        def _(b):
            rows = pl.ds(pl.multiple_of(b * BS, BS), BS)
            kb = kinds[1, b]
            odd = (kb & 1) == 1
            v = jnp.where(kb < 2, acc[rows, 0:LANES], acc[rows, LANES : 2 * LANES])
            r = pltpu.roll(v, BS, 1)
            evens = jnp.where(odd, r[:pairs], v[:pairs])
            odds = jnp.where(odd, v[pairs:], r[pairs:])
            block = jnp.where(low, evens, odds)
            if h == 0:
                out_ref[b] = block
            else:
                vn[b] = block + other_ref[b]

        if h == 1:
            out_ref[...] = vn[...].reshape(NB, BS * BS).astype(BF16)


def make_tiles(h, small, density_blocks, basis):
    width = 2 * HALF + (LANES if h == 0 else 0)
    return pl.pallas_call(
        lambda *refs: tiles_kernel(h, *refs),
        grid=(STEPS,),
        in_specs=[SMEM] * len(small) + [whole((NB, BS * BS))] + basis_specs(h),
        out_specs=[whole((DEVS * CZB, width))] + [SMEM, moved_spec()] * h,
        out_shape=[jax.ShapeDtypeStruct((DEVS * CZB, width), BF16)]
        + [
            jax.ShapeDtypeStruct((NB,), jnp.int32),
            jax.ShapeDtypeStruct((STEPS, KINDS * BS, SEGW), BF16),
        ]
        * h,
        scratch_shapes=[
            pltpu.VMEM((NB, BS // 2, LANES), F32),
            pltpu.VMEM((NB * BS, KINDS * BS), BF16),
            pltpu.VMEM((KINDS * BS, SEGW), F32),
            pltpu.VMEM((KINDS * BS, KINDS * BS), BF16),
            pltpu.VMEM(((NB + 1) * CZB, HALF), F32),
            pltpu.SMEM((2 * DEVS,), jnp.int32),
        ],
        cost_estimate=cost(2 * NB * BS * KINDS * BS * CZB * HALF, 4 << 20),
        compiler_params=room(TILES_MIB),
    )(*small, density_blocks, basis, basis)


def gather_tiles(h, got, ext_potential, places=None):
    part = jax.ShapeDtypeStruct((CZB, PLANE // HALVES), F32)
    swap = jax.ShapeDtypeStruct((CZB, PLANE // HALVES), BF16)
    acc = pltpu.VMEM((SEGS * LPS * 2 * CZB, LANES), F32)
    if h == 0:
        return pl.pallas_call(
            gather_first,
            in_specs=[VMEM, VMEM],
            out_specs=[VMEM, VMEM, VMEM, VMEM, SMEM],
            out_shape=[part, part, swap, swap, jax.ShapeDtypeStruct((8, DEVS), jnp.int32)],
            scratch_shapes=[
                pltpu.VMEM((DEVS * CZB, LANES), F32),
                pltpu.VMEM((8, DEVS), jnp.int32),
                acc,
                pltpu.SemaphoreType.DMA,
            ],
            cost_estimate=cost(1 << 20, 3 << 20),
            compiler_params=room(SMALL_MIB),
            name="gather_tiles0",
        )(got, ext_potential)
    return pl.pallas_call(
        gather_second,
        in_specs=[SMEM, VMEM, VMEM],
        out_specs=[VMEM, VMEM, VMEM, VMEM],
        out_shape=[part, part, swap, swap],
        scratch_shapes=[acc],
        cost_estimate=cost(1 << 20, 3 << 20),
        compiler_params=room(SMALL_MIB),
        name="gather_tiles1",
    )(places, got, ext_potential)


def cut_cubes(h, places, own, rim, ext_potential, near, far, *other):
    width = PLANE // HALVES if h == 0 else PLANE
    return pl.pallas_call(
        lambda *refs: cubes_kernel(h, *refs),
        in_specs=[SMEM] + [VMEM] * (5 + len(other)),
        out_specs=[VMEM, VMEM],
        out_shape=[
            jax.ShapeDtypeStruct((CZB, width), F32),
            jax.ShapeDtypeStruct((DEVS * 16, HALF), BF16),
        ],
        scratch_shapes=[pltpu.VMEM((SEGS * LPS * 2 * CZB, LANES), F32)],
        cost_estimate=cost(1 << 20, 3 << 20),
        compiler_params=room(SMALL_MIB),
    )(places, own, rim, ext_potential, near, far, *other)


def make_matrices(h, base, kinds, returned, basis, *other):
    blocks = (NB, BS // 2, LANES)
    out = (blocks, F32) if h == 0 else ((NB, BS * BS), BF16)
    return pl.pallas_call(
        lambda *refs: matrix_kernel(h, *refs),
        grid=(STEPS,),
        in_specs=[SMEM, SMEM, whole((DEVS * 16, HALF))]
        + basis_specs(h)
        + [whole(blocks), moved_spec()] * h,
        out_specs=whole(out[0]),
        out_shape=jax.ShapeDtypeStruct(*out),
        scratch_shapes=[
            pltpu.VMEM((NB * BS, KINDS * BS), F32),
            pltpu.VMEM((DEVS * 16, HALF), F32),
        ]
        + [
            pltpu.VMEM((KINDS * BS, KINDS * BS), BF16),
            pltpu.VMEM((KINDS * BS, SEGW), BF16),
        ]
        * (1 - h)
        + [pltpu.VMEM(blocks, F32)] * h,
        cost_estimate=cost(2 * NB * BS * KINDS * BS * CZB * HALF, 4 << 20),
        compiler_params=room(MATRICES_MIB),
    )(base, kinds, returned, basis, basis, *other)


def swapped(near, far):
    pairs = [(home(e), home(e ^ 1)) for e in range(DEVS)]
    next_pairs = [(home(e), home((((e + 1) ^ 1) - 1) % DEVS)) for e in range(DEVS)]
    return lax.ppermute(near, AXES, pairs), lax.ppermute(far, AXES, next_pairs)


def copy_kernel(in_ref, out_ref):
    out_ref[...] = in_ref[...]


def written(x):
    return pl.pallas_call(
        copy_kernel,
        in_specs=[VMEM],
        out_specs=VMEM,
        out_shape=jax.ShapeDtypeStruct(x.shape, x.dtype),
        compiler_params=room(SMALL_MIB),
        cost_estimate=cost(1 << 10, 1 << 18),
        name="written",
    )(x)


def to_homes(x):
    return lax.ppermute(x, AXES, [(e, home(e)) for e in range(DEVS)])


def from_homes(x):
    return lax.ppermute(x, AXES, [(home(e), e) for e in range(DEVS)])


def exchanged(x):
    return lax.all_to_all(x, AXES, split_axis=0, concat_axis=0, tiled=True)


def local(
    density_blocks, block_owner, block_plane, block_segment, block_kinds, basis, ext_potential
):
    owner, kinds = block_owner.T, block_kinds.T
    ext_potential = to_homes(ext_potential)
    small = (owner, kinds)
    (sent0,) = make_tiles(0, small + (block_plane, block_segment), density_blocks, basis)
    sent1, base, moved = make_tiles(1, small, density_blocks, basis)
    got = [exchanged(sent0), exchanged(sent1)]

    own, rim, near, far, places = gather_tiles(0, got[0], ext_potential)
    near, far = swapped(near, far)
    density, cubes = cut_cubes(0, places, own, rim, ext_potential, near, far)
    returned0 = exchanged(cubes)

    own, rim, near, far = gather_tiles(1, got[1], ext_potential, places)
    near, far = swapped(near, far)
    density, cubes = cut_cubes(1, places, own, rim, ext_potential, near, far, density)
    returned1 = exchanged(cubes)
    density = from_homes(density)

    density = written(density)
    partial = make_matrices(0, base, kinds, returned0, basis)
    matrices = make_matrices(1, base, kinds, returned1, basis, partial, moved)
    return density, matrices


def solution(mesh):
    rows = P(AXES, None)
    flat = P(AXES)
    return jax.shard_map(
        local,
        mesh=mesh,
        in_specs=(rows, rows, flat, flat, rows, P(), rows),
        out_specs=(rows, rows),
        check_vma=False,
    )
```
